256 devices in a mesh: dp: 32 (over y, z), tensor: 8 (over x, core).
Axes of the slice: x: 4, y: 4, z: 8, core: 2. Of those that a mesh axis runs over, the one named last changes fastest.
Arguments:
- tokens: bfloat16 [4096, 8192], P(('dp', 'tensor')), may hold values from -6 to 6
- base_weight: bfloat16 [8192, 4096], P(None, 'tensor'), may hold values from -0.0625 to 0.0625
- out_grad: bfloat16 [4096, 4096], P('dp', 'tensor'), may hold values from -6 to 6
- block_index: int32 [32, 2], replicated, may hold values from 0 to 63, as said below
- block_owner: int32 [32], replicated, may hold values from 0 to 31, as said below
- delta: bfloat16 [64, 16384], P('dp', 'tensor'), may hold values from -0.5 to 0.5
- moment1: float32 [64, 16384], P('dp', 'tensor'), may hold values from -4 to 4
- moment2: float32 [64, 16384], P('dp', 'tensor'), may hold values from 0.01 to 1
Outputs:
- projected: bfloat16 [4096, 4096], P('dp', 'tensor')
- input_grad: bfloat16 [4096, 8192], P(('dp', 'tensor'))
- new_delta: bfloat16 [64, 16384], P('dp', 'tensor')
- new_moment1: float32 [64, 16384], P('dp', 'tensor')
- new_moment2: float32 [64, 16384], P('dp', 'tensor')
The draws below stay inside these ranges and needn't reach their ends.
Inputs may be any that keep to these rules, and one draw needn't show every extreme that they name: `block_index`: the pairs (row block, head) are all different; row blocks are below D / 128 and heads below 32. `block_owner`: each owner holds at most 2 blocks and some owner exactly 2; some owners hold none.
All inputs are finite; a program needn't handle non-finite values.
Results may differ from the reference program's by a relative error of at most 0.013.
Values may be sent and summed in bfloat16 or wider, within the bound.
A program may use at most 128 MiB of HBM per device.

```python
import math
import jax
import jax.numpy as jnp
from jax import lax

D = 8192
HEAD_DIM = 128
HEADS = 32
BPO = 1
CAP = 2
NB = 32
SLOTS = 64
TOKENS = 4096
N_DP = 32
N_TENSOR = 8


def move_front(order, target, place):
    cells = order.shape[0]
    where_now = jnp.sum(jnp.where(order == target, jnp.arange(cells, dtype=jnp.int32), 0)).astype(jnp.int32)
    held = order[place]
    order = order.at[where_now].set(held)
    return order.at[place].set(target)


def draw_block_index(key, part):
    cells = D // HEAD_DIM * HEADS
    order = jax.random.permutation(jax.random.fold_in(key, 11), cells).astype(jnp.int32)
    far_cell = jnp.int32(cells - 1)
    near_cell = jnp.int32(0)
    order = move_front(order, far_cell, 0)
    order = move_front(order, near_cell, 1)
    order = order[:NB]
    return jnp.stack([order // HEADS, order % HEADS], axis=1).astype(jnp.int32)


def draw_block_owner(key, part):
    owners = jnp.arange(N_DP, dtype=jnp.int32)
    phase = owners % 4
    counts = jnp.where(phase == 0, 2 * BPO, jnp.where(phase == 3, 0, BPO))
    sorted_owner = jnp.repeat(owners, counts, total_repeat_length=NB)
    relabel = jax.random.permutation(jax.random.fold_in(key, 21), N_DP)
    shuffle = jax.random.permutation(jax.random.fold_in(key, 22), NB)
    return relabel[sorted_owner][shuffle].astype(jnp.int32)


def levels(key, dims, cuts, smallest, top_value):
    def one(axis_at, shards_of):
        draws = jax.random.uniform(jax.random.fold_in(jax.random.fold_in(key, 6), axis_at), (shards_of,), jnp.float32, smallest / len(cuts), top_value / len(cuts))
        return jnp.repeat(jnp.exp(draws), dims[axis_at] // shards_of).reshape((-1,) + (1,) * (len(dims) - axis_at - 1))

    level = one(*cuts[0])
    for cut in cuts[1:]:
        level = level * one(*cut)
    return level


def centred(own_key, shape, width, reach, cuts=(), kind=jnp.bfloat16):
    factor_of = levels(own_key, shape, cuts, -0.22, 0.18) if cuts else 1.0
    entries = jax.random.normal(own_key, shape, jnp.float32) * width * factor_of
    return jnp.minimum(jnp.maximum(entries, -reach), reach).astype(kind)


def setup_inputs(seed: int = 0) -> dict:
    key_list = jax.random.split(jax.random.key(seed), 9)
    return {
        "tokens": centred(key_list[0], (TOKENS, D), 1.0, 6.0, ((0, 256),)),
        "base_weight": centred(key_list[1], (D, HEADS * HEAD_DIM), D ** -0.5, 0.0625, ((1, 8),)),
        "out_grad": centred(key_list[2], (TOKENS, HEADS * HEAD_DIM), 1.0, 6.0, ((0, 32), (1, 8))),
        "block_index": draw_block_index(jax.random.fold_in(key_list[8], 71), 0),
        "block_owner": draw_block_owner(jax.random.fold_in(key_list[8], 71), 0),
        "delta": centred(key_list[5], (SLOTS, HEAD_DIM * HEAD_DIM), HEAD_DIM ** -0.5, 0.5, ((0, 32), (1, 8))),
        "moment1": centred(key_list[6], (SLOTS, HEAD_DIM * HEAD_DIM), 0.5, 4.0, ((0, 32), (1, 8)), jnp.float32),
        "moment2": jnp.clip(jnp.exp(math.log(1.0) - 4.6051702 * jax.random.uniform(key_list[7], (SLOTS, HEAD_DIM * HEAD_DIM), jnp.float32) ** levels(key_list[7], (SLOTS, HEAD_DIM * HEAD_DIM), ((0, 32), (1, 8)), -0.2, 0.2)), 0.01, 1.0),
    }


CORRECT_ONE = 1.0 - 0.9 ** 10
CORRECT_TWO = 1.0 - 0.999 ** 10

def tables(block_index, block_owner):
    owners = jnp.arange(N_DP, dtype=jnp.int32)
    owner_hit = (block_owner[:, None] == owners[None, :]).astype(jnp.int32)
    before = jnp.cumsum(owner_hit, axis=0) - owner_hit
    slot_rank = lax.optimization_barrier(jnp.sum(before * owner_hit, axis=1))
    slot_of = block_owner * CAP + slot_rank
    slot_match = (slot_of[None, :] == jnp.arange(SLOTS, dtype=jnp.int32)[:, None]).astype(jnp.int32)
    slot_live = lax.optimization_barrier(jnp.sum(slot_match, axis=1))
    slot_row = lax.optimization_barrier(jnp.sum(slot_match * block_index[None, :, 0], axis=1))
    slot_head = lax.optimization_barrier(jnp.sum(slot_match * block_index[None, :, 1], axis=1))
    return (slot_live, slot_row, slot_head)

def reference(tokens, base_weight, out_grad, block_index, block_owner, delta, moment1, moment2):
    slot_live, slot_row, slot_head = tables(block_index, block_owner)
    blocks = delta.reshape(SLOTS, HEAD_DIM, HEAD_DIM)
    base_part = jnp.dot(tokens, base_weight, preferred_element_type=jnp.float32)

    def add_forward(slot_index, running):
        token_slab = lax.dynamic_slice_in_dim(tokens, slot_row[slot_index] * HEAD_DIM, HEAD_DIM, 1)
        delta_term = jnp.dot(token_slab, blocks[slot_index], preferred_element_type=jnp.float32)
        delta_term = delta_term * slot_live[slot_index].astype(jnp.float32)
        column = slot_head[slot_index] * HEAD_DIM
        current = lax.dynamic_slice_in_dim(running, column, HEAD_DIM, 1)
        return lax.dynamic_update_slice_in_dim(running, current + delta_term, column, 1)
    projected = lax.fori_loop(0, SLOTS, add_forward, base_part).astype(jnp.bfloat16)
    heads_dev = HEADS // N_TENSOR
    width_dev = heads_dev * HEAD_DIM
    total = jnp.zeros((TOKENS, D), jnp.float32)
    for shard_index in range(N_TENSOR):
        grad_cols = out_grad[:, shard_index * width_dev:(shard_index + 1) * width_dev]
        weight_cols = base_weight[:, shard_index * width_dev:(shard_index + 1) * width_dev]
        base_back = lax.dot_general(grad_cols, weight_cols, (((1,), (1,)), ((), ())), preferred_element_type=jnp.float32)

        def add_back(slot_index, running):

            def update(state):
                grad_slab = lax.dynamic_slice_in_dim(out_grad, slot_head[slot_index] * HEAD_DIM, HEAD_DIM, 1)
                delta_term = lax.dot_general(grad_slab, blocks[slot_index], (((1,), (1,)), ((), ())), preferred_element_type=jnp.float32)
                row_start = slot_row[slot_index] * HEAD_DIM
                current = lax.dynamic_slice_in_dim(state, row_start, HEAD_DIM, 1)
                return lax.dynamic_update_slice_in_dim(state, current + delta_term, row_start, 1)
            owned = jnp.logical_and(slot_live[slot_index] > 0, slot_head[slot_index] // heads_dev == shard_index)
            return lax.cond(owned, update, lambda state: state, running)
        base_back = lax.fori_loop(0, SLOTS, add_back, base_back)
        rounded = lax.optimization_barrier(base_back.astype(jnp.bfloat16))
        total = total + rounded.astype(jnp.float32)
    input_grad = total.astype(jnp.bfloat16)
    grad_scale = 1.0 / math.sqrt(TOKENS)

    def grad_one(slot_index):
        token_slab = lax.dynamic_slice_in_dim(tokens, slot_row[slot_index] * HEAD_DIM, HEAD_DIM, 1)
        grad_slab = lax.dynamic_slice_in_dim(out_grad, slot_head[slot_index] * HEAD_DIM, HEAD_DIM, 1)
        grad_block = lax.dot_general(token_slab, grad_slab, (((0,), (0,)), ((), ())), preferred_element_type=jnp.float32)
        weight_live = slot_live[slot_index].astype(jnp.float32) * grad_scale
        return (grad_block * weight_live).reshape(HEAD_DIM * HEAD_DIM)
    block_grad = lax.map(grad_one, jnp.arange(SLOTS, dtype=jnp.int32))
    first_new = 0.9 * moment1 + 0.1 * block_grad
    second_new = 0.999 * moment2 + 0.001 * block_grad * block_grad
    update_step = 0.02 * (first_new / CORRECT_ONE) / (jnp.sqrt(second_new / CORRECT_TWO) + 1e-08)
    new_delta = (delta.astype(jnp.float32) - update_step).astype(jnp.bfloat16)
    return (projected, input_grad, new_delta, first_new, second_new)
```

```python
import math

import jax
import jax.numpy as jnp
from jax import lax
from jax.experimental import pallas as pl
from jax.experimental.pallas import tpu as pltpu
from jax.sharding import PartitionSpec as P

D = 8192
HD = 128
NB = 32
CAP = 2
NX = 4
ROWS = 16
TOK = 128
WIDTH = 512
HEADS_DEV = 4
CHUNKS = 8
CW = D // CHUNKS

CORRECT_ONE = 1.0 - 0.9**10
CORRECT_TWO = 1.0 - 0.999**10

SLOT = 0
ROW = 32
HEAD = 64
BLK = 96
INV = 160
TAB = 512

F32 = jnp.float32
BF16 = jnp.bfloat16


def table_kernel(slots, index, owner, tab, count):
    t = lax.axis_index("tensor")

    def clear(i, _):
        tab[INV + i] = NB
        return 0

    lax.fori_loop(0, 4 * D // HD + 1, clear, 0, unroll=8)

    def clear_slot(i, _):
        tab[BLK + i] = NB
        count[i] = 0
        return 0

    lax.fori_loop(0, slots, clear_slot, 0, unroll=8)

    def place(b, _):
        o = owner[b]
        rank = count[o]
        count[o] = rank + 1
        slot = o * CAP + rank
        row = index[b, 0]
        head = index[b, 1]
        tab[SLOT + b] = slot
        tab[ROW + b] = row
        tab[HEAD + b] = head
        tab[BLK + slot] = b
        local = head - t * HEADS_DEV
        mine = jnp.logical_and(local >= 0, local < HEADS_DEV)
        tab[INV + jnp.where(mine, row * HEADS_DEV + local, 4 * D // HD)] = b
        return 0

    lax.fori_loop(0, NB, place, 0)


def step_kernel(
    ny, nz, grad_scale,
    tab, tok, wt, og, dl, m1, m2,
    proj, ig, nd, nm1, nm2,
    wv, tokf, tok3, ogf, og3, ogp, dsl, dcp, gtmp, gc, gsl, gy, gys, gz, acc,
    pown, sibs, sibr, s1s, s1r, s2s, s2r, qs, qr, ql,
    wsem, lsem, ags, agr, zs, zr, ys, yr, gys_s, gys_r, gzs, gzr, rss, rsr,
):
    d = lax.axis_index("dp")
    t = lax.axis_index("tensor")
    y, z = lax.div(d, nz), lax.rem(d, nz)
    x, c = lax.div(t, 2), lax.rem(t, 2)

    def at(dx, core):
        return lax.rem(x + dx, NX) * 2 + core

    t_right, t_left, t_opp, t_sib = at(1, c), at(3, c), at(2, c), at(0, 1 - c)

    def z_peer(i):
        return y * nz + lax.rem(z + i, nz)

    def y_peer(i):
        return lax.rem(y + i, ny) * nz + z

    def remote(src, dst, send, recv, **where):
        return pltpu.make_async_remote_copy(
            src_ref=src, dst_ref=dst, send_sem=send, recv_sem=recv,
            device_id=where, device_id_type=pl.DeviceIdType.MESH,
        )

    w_copies = [
        pltpu.make_async_copy(
            wt.at[pl.ds(j * CW, CW), :], wv.at[pl.ds(j * CW, CW), :], wsem.at[j]
        )
        for j in range(CHUNKS)
    ]
    for copy in w_copies:
        copy.start()
    own_og = pltpu.make_async_copy(og, ogf.at[t], lsem.at[0])
    own_og.start()
    own_tok = pltpu.make_async_copy(tok, tokf.at[pl.ds(t * ROWS, ROWS), :], lsem.at[1])
    own_tok.start()

    entries = dl[...].astype(F32)
    for s in range(CAP):
        rows = [entries[s : s + 1, i * HD : (i + 1) * HD] for i in range(ROWS)]
        dsl[CAP * d + s] = jnp.concatenate(rows, axis=0).astype(BF16)
    for k in range(2 * NX):
        dcp[k, NB] = jnp.zeros((ROWS, HD), BF16)
    gc[NB] = jnp.zeros((ROWS, HD), F32)

    barrier = pltpu.get_barrier_semaphore()
    near = [{"tensor": t_right}, {"tensor": t_left}, {"tensor": t_sib}]
    near += [{"dp": z_peer(i)} for i in range(1, nz)]
    near += [{"dp": y_peer(i)} for i in range(1, ny)]
    for where in near:
        pl.semaphore_signal(
            barrier, inc=1, device_id=where, device_id_type=pl.DeviceIdType.MESH
        )
    pl.semaphore_wait(barrier, len(near))

    def shard(q, k):
        if q < 2:
            return ogf.at[k, pl.ds(64 * q, 64), :]
        if q < 6:
            return tokf.at[pl.ds(k * ROWS, ROWS), pl.ds(2048 * (q - 2), 2048)]
        return dcp.at[k, pl.ds(16 * (q - 6), 16)]

    def mine(q):
        if q < 2:
            return og.at[pl.ds(64 * q, 64), :]
        if q < 6:
            return tok.at[:, pl.ds(2048 * (q - 2), 2048)]
        return shard(q, t)

    def ag(q, kind):
        sems = (ags.at[q, kind], agr.at[q, kind])
        if kind == 0:
            return remote(mine(q), shard(q, t), *sems, tensor=t_right)
        if kind == 1:
            return remote(mine(q), shard(q, t), *sems, tensor=t_left)
        if kind == 2:
            return remote(mine(q), shard(q, t), *sems, tensor=t_sib)
        if kind == 3:
            return remote(shard(q, t_left), shard(q, t_left), *sems, tensor=t_sib)
        if kind == 4:
            return remote(shard(q, t_right), shard(q, t_right), *sems, tensor=t_sib)
        if kind == 5 and q % 2 == 0:
            return remote(shard(q, t_left), shard(q, t_left), *sems, tensor=t_right)
        if kind == 5:
            return remote(shard(q, t_right), shard(q, t_right), *sems, tensor=t_left)
        return remote(shard(q, t_opp), shard(q, t_opp), *sems, tensor=t_sib)

    def ag_own(q):
        for kind in range(3):
            ag(q, kind).start()

    def ag_pass(q):
        ag(q, 0).wait_recv()
        if q % 2 == 0:
            ag(q, 5).start()
        ag(q, 3).start()
        ag(q, 1).wait_recv()
        if q % 2 == 1:
            ag(q, 5).start()
        ag(q, 4).start()

    def ag_last(q):
        ag(q, 5).wait_recv()
        ag(q, 6).start()

    def ag_end(q):
        for kind in (2, 3, 4, 6):
            ag(q, kind).wait_recv()

    def zcopy(i):
        part = dsl.at[pl.ds(CAP * d, CAP)]
        return remote(part, part, zs.at[i - 1], zr.at[i - 1], dp=z_peer(i))

    def ycopy(i):
        part = dsl.at[pl.ds(CAP * nz * y, CAP * nz)]
        return remote(part, part, ys.at[i - 1], yr.at[i - 1], dp=y_peer(i))

    for i in range(1, nz):
        zcopy(i).start()
    for q in range(6):
        ag_own(q)

    own_og.wait()
    order = [at(dx, core) for core in (c, 1 - c) for dx in (0, 1, 3, 2)]
    for i, k in enumerate(order):
        ogp[pl.ds(i * ROWS, ROWS), :] = ogf[t, pl.ds(pl.multiple_of(k * ROWS, ROWS), ROWS), :]

    ag_pass(0)
    ag_pass(1)
    for i in range(1, nz):
        zcopy(i).wait_recv()
    for i in range(1, ny):
        ycopy(i).start()
    ag_last(0)
    ag_last(1)
    ag_pass(2)
    ag_pass(3)
    for i in range(1, ny):
        ycopy(i).wait_recv()
    for b in range(NB):
        dcp[t, b] = dsl[tab[SLOT + b]]
    ag_own(6)
    ag_own(7)
    ag_last(2)
    ag_last(3)
    ag_pass(4)
    ag_pass(5)
    ag_last(4)
    ag_last(5)
    own_tok.wait()
    for q in range(6):
        ag_end(q)

    def grad_block(b, _):
        gtmp[b] = lax.dot_general(
            tok3[tab[ROW + b]], og3[tab[HEAD + b]], (((0,), (0,)), ((), ())),
            preferred_element_type=F32,
        )
        return 0

    for r in range(D // HD):
        tok3[r] = tokf[:, r * HD : (r + 1) * HD]
    for h in range(2 * NX * HEADS_DEV):
        col = h % HEADS_DEV * HD
        og3[h] = ogf[h // HEADS_DEV, :, col : col + HD]

    lax.fori_loop(0, NB // 2, grad_block, 0)
    ag_pass(6)
    ag_pass(7)
    lax.fori_loop(NB // 2, NB, grad_block, 0)

    def grad_rows(b, _):
        gc[b] = gtmp[b, pl.ds(pl.multiple_of(t * ROWS, ROWS), ROWS), :] * grad_scale
        return 0

    lax.fori_loop(0, NB, grad_rows, 0, unroll=4)
    for s in range(CAP * ny * nz):
        gsl[s] = gc[tab[BLK + s]].astype(BF16)

    def gycopy(i):
        return remote(
            gsl.at[pl.ds(CAP * nz * lax.rem(y + i, ny), CAP * nz)],
            gy.at[i - 1], gys_s.at[i - 1], gys_r.at[i - 1], dp=y_peer(i),
        )

    def gzcopy(i):
        return remote(
            gys.at[pl.ds(CAP * lax.rem(z + i, nz), CAP)],
            gz.at[i - 1], gzs.at[i - 1], gzr.at[i - 1], dp=z_peer(i),
        )

    for i in range(1, ny):
        gycopy(i).start()
    ag_last(6)
    ag_last(7)
    ag_end(6)
    ag_end(7)
    for copy in w_copies:
        copy.wait()

    half = CW // 2

    def rs_sib(j):
        return remote(sibs.at[j], sibr.at[j], rss.at[j, 0], rsr.at[j, 0], tensor=t_sib)

    def rs_one(j):
        return (
            remote(s1s.at[j, 0], s1r.at[j, 0], rss.at[j, 1], rsr.at[j, 1], tensor=t_right),
            remote(s1s.at[j, 1], s1r.at[j, 1], rss.at[j, 2], rsr.at[j, 2], tensor=t_left),
        )

    def rs_two(j):
        return (
            remote(s2s.at[j, 0], s2r.at[j, 0], rss.at[j, 3], rsr.at[j, 3], tensor=t_right),
            remote(s2s.at[j, 1], s2r.at[j, 1], rss.at[j, 4], rsr.at[j, 4], tensor=t_left),
        )

    acc[...] = jnp.zeros_like(acc)

    def reduce_step(i, _):
        @pl.when(i < CHUNKS)
        def _():
            def patch(rb, _):
                block_row = i * (CW // HD) + rb
                base = pl.multiple_of(block_row * HD, HD)
                for h in range(HEADS_DEV):
                    b = tab[INV + block_row * HEADS_DEV + h]
                    for k in range(2 * NX):
                        here = (pl.ds(base + k * ROWS, ROWS), pl.ds(h * HD, HD))
                        wv[here] = (wv[here].astype(F32) + dcp[k, b].astype(F32)).astype(BF16)
                return 0

            lax.fori_loop(0, CW // HD, patch, 0)
            rows = pl.ds(pl.multiple_of(i * CW, CW), CW)
            part = lax.dot_general(
                ogp[...], wv[rows, :], (((1,), (1,)), ((), ())), preferred_element_type=F32
            )
            sibs[i] = part[4 * ROWS :].astype(BF16)
            pown[i] = part[: 4 * ROWS]
            rs_sib(i).start()

        @pl.when(jnp.logical_and(i >= 1, i < CHUNKS + 1))
        def _():
            j = i - 1
            rs_sib(j).wait_recv()
            total = pown[j] + sibr[j].astype(F32)
            qs[j] = total[:ROWS]
            qr[j] = total[ROWS : 2 * ROWS]
            ql[j] = total[2 * ROWS : 3 * ROWS]
            far = total[3 * ROWS :].astype(BF16)
            s1s[j, 0] = far[:, :half]
            s1s[j, 1] = far[:, half:]
            for copy in rs_one(j):
                copy.start()

        @pl.when(jnp.logical_and(i >= 2, i < CHUNKS + 2))
        def _():
            j = i - 2
            for copy in rs_one(j):
                copy.wait_recv()
            s2s[j, 0, :, :half] = (qr[j, :, :half] + s1r[j, 0].astype(F32)).astype(BF16)
            s2s[j, 0, :, half:] = qr[j, :, half:].astype(BF16)
            s2s[j, 1, :, :half] = ql[j, :, :half].astype(BF16)
            s2s[j, 1, :, half:] = (ql[j, :, half:] + s1r[j, 1].astype(F32)).astype(BF16)
            for copy in rs_two(j):
                copy.start()

        @pl.when(i < CHUNKS)
        def _():
            rows = pl.ds(pl.multiple_of(i * CW, CW), CW)
            acc[...] += jnp.dot(tokf[:, rows], wv[rows, :], preferred_element_type=F32)

        @pl.when(i >= 3)
        def _():
            j = i - 3
            for copy in rs_two(j):
                copy.wait_recv()
            out = qs[j] + s2r[j, 0].astype(F32) + s2r[j, 1].astype(F32)
            ig[:, pl.ds(pl.multiple_of(j * CW, CW), CW)] = out.astype(BF16)

        return 0

    lax.fori_loop(0, CHUNKS // 2, reduce_step, 0)

    for i in range(1, ny):
        gycopy(i).wait_recv()
    for s in range(CAP * nz):
        total = gsl[CAP * nz * y + s].astype(F32)
        for i in range(ny - 1):
            total = total + gy[i, s].astype(F32)
        gys[s] = total.astype(BF16)
    for i in range(1, nz):
        gzcopy(i).start()

    lax.fori_loop(CHUNKS // 2, CHUNKS + 3, reduce_step, 0)
    proj[...] = acc[...].astype(BF16)

    for i in range(1, nz):
        gzcopy(i).wait_recv()
    grads = []
    for s in range(CAP):
        total = gys[CAP * z + s].astype(F32)
        for i in range(nz - 1):
            total = total + gz[i, s].astype(F32)
        grads.append(jnp.concatenate([total[i : i + 1] for i in range(ROWS)], axis=1))
    grad = jnp.concatenate(grads, axis=0)
    first = 0.9 * m1[...] + 0.1 * grad
    second = 0.999 * m2[...] + 0.001 * grad * grad
    step = 0.02 * (first / CORRECT_ONE) / (jnp.sqrt(second / CORRECT_TWO) + 1e-08)
    nm1[...] = first
    nm2[...] = second
    nd[...] = (dl[...].astype(F32) - step).astype(BF16)

    for i in range(1, nz):
        zcopy(i).wait_send()
        gzcopy(i).wait_send()
    for i in range(1, ny):
        ycopy(i).wait_send()
        gycopy(i).wait_send()
    for q in range(8):
        for kind in range(7):
            ag(q, kind).wait_send()

    def drain(j, _):
        for copy in (rs_sib(j), *rs_one(j), *rs_two(j)):
            copy.wait_send()
        return 0

    lax.fori_loop(0, CHUNKS, drain, 0)


def on_device(ny, nz, tokens, base_weight, out_grad, block_index, block_owner, delta, moment1, moment2):
    slots = CAP * ny * nz
    smem = pl.BlockSpec(memory_space=pltpu.SMEM)
    vmem = pl.BlockSpec(memory_space=pltpu.VMEM)
    hbm = pl.BlockSpec(memory_space=pl.ANY)

    tab = pl.pallas_call(
        lambda *refs: table_kernel(slots, *refs),
        out_shape=jax.ShapeDtypeStruct((TAB,), jnp.int32),
        in_specs=[smem, smem],
        out_specs=smem,
        scratch_shapes=[pltpu.SMEM((64,), jnp.int32)],
        name="tables",
    )(block_index, block_owner)

    dma = pltpu.SemaphoreType.DMA
    grad_scale = 1.0 / math.sqrt(TOK * ny * nz)
    half = CW // 2
    return pl.pallas_call(
        lambda *refs: step_kernel(ny, nz, grad_scale, *refs),
        out_shape=(
            jax.ShapeDtypeStruct((TOK, WIDTH), BF16),
            jax.ShapeDtypeStruct((ROWS, D), BF16),
            jax.ShapeDtypeStruct(delta.shape, BF16),
            jax.ShapeDtypeStruct(delta.shape, F32),
            jax.ShapeDtypeStruct(delta.shape, F32),
        ),
        in_specs=[smem, hbm, hbm, hbm, vmem, vmem, vmem],
        out_specs=(vmem,) * 5,
        scratch_shapes=[
            pltpu.VMEM((D, WIDTH), BF16),
            pltpu.VMEM((TOK, D), BF16),
            pltpu.VMEM((D // HD, TOK, HD), BF16),
            pltpu.VMEM((2 * NX, TOK, WIDTH), BF16),
            pltpu.VMEM((2 * NX * HEADS_DEV, TOK, HD), BF16),
            pltpu.VMEM((TOK, WIDTH), BF16),
            pltpu.VMEM((slots, ROWS, HD), BF16),
            pltpu.VMEM((2 * NX, NB + 1, ROWS, HD), BF16),
            pltpu.VMEM((NB, HD, HD), F32),
            pltpu.VMEM((NB + 1, ROWS, HD), F32),
            pltpu.VMEM((slots, ROWS, HD), BF16),
            pltpu.VMEM((ny - 1, CAP * nz, ROWS, HD), BF16),
            pltpu.VMEM((CAP * nz, ROWS, HD), BF16),
            pltpu.VMEM((nz - 1, CAP, ROWS, HD), BF16),
            pltpu.VMEM((TOK, WIDTH), F32),
            pltpu.VMEM((CHUNKS, 4 * ROWS, CW), F32),
            pltpu.VMEM((CHUNKS, 4 * ROWS, CW), BF16),
            pltpu.VMEM((CHUNKS, 4 * ROWS, CW), BF16),
            pltpu.VMEM((CHUNKS, 2, ROWS, half), BF16),
            pltpu.VMEM((CHUNKS, 2, ROWS, half), BF16),
            pltpu.VMEM((CHUNKS, 2, ROWS, CW), BF16),
            pltpu.VMEM((CHUNKS, 2, ROWS, CW), BF16),
            pltpu.VMEM((CHUNKS, ROWS, CW), F32),
            pltpu.VMEM((CHUNKS, ROWS, CW), F32),
            pltpu.VMEM((CHUNKS, ROWS, CW), F32),
            dma((CHUNKS,)),
            dma((2,)),
            dma((8, 7)),
            dma((8, 7)),
            dma((nz - 1,)),
            dma((nz - 1,)),
            dma((ny - 1,)),
            dma((ny - 1,)),
            dma((ny - 1,)),
            dma((ny - 1,)),
            dma((nz - 1,)),
            dma((nz - 1,)),
            dma((CHUNKS, 5)),
            dma((CHUNKS, 5)),
        ],
        compiler_params=pltpu.CompilerParams(
            collective_id=0, has_side_effects=True, vmem_limit_bytes=50 * 1024 * 1024
        ),
        name="step",
    )(tab, tokens, base_weight, out_grad, delta, moment1, moment2)


def solution(mesh):
    dp = mesh.shape["dp"]
    nz = 8
    ny = dp // nz

    def per_device(*args):
        return on_device(ny, nz, *args)

    both = P("dp", "tensor")
    rows = P(("dp", "tensor"), None)
    return jax.shard_map(
        per_device,
        mesh=mesh,
        in_specs=(rows, P(None, "tensor"), both, P(), P(), both, both, both),
        out_specs=(both, rows, both, both, both),
        check_vma=False,
    )
```

```python
import math

import jax
import jax.numpy as jnp
from jax import lax
from jax.experimental import pallas as pl
from jax.experimental.pallas import tpu as pltpu
from jax.sharding import PartitionSpec as P

D = 8192
HD = 128
NB = 32
CAP = 2
NX = 4
NT = 8
ROWS = 16
TOK = 128
WIDTH = 512
HEADS_DEV = 4
CHUNKS = 8
CW = D // CHUNKS
HALF = CW // 2
KB = 8

CORRECT_ONE = 1.0 - 0.9**10
CORRECT_TWO = 1.0 - 0.999**10

F32 = jnp.float32
BF16 = jnp.bfloat16
MESH = pl.DeviceIdType.MESH


def step_kernel(
    ny, nz, grad_scale,
    index_in, owner_in, tok, wt, og, dl,
    igb, udel, proj, grad_out,
    wv, tokf, tok3, ogf, og3, og16, ogp, dlv, dsl, dcp, gc, gsl, gy, gys, gz,
    pown, sibs, sibr, s1s, s1r, s2s, s2r, qs, qr, ql, lhs, rhs, blkv, blk, slot, index, owner,
    wsem, lsem, snd, agr, sbr, dpr, rsr, known,
):
    d = lax.axis_index("dp")
    t = lax.axis_index("tensor")
    y, z = lax.div(d, nz), lax.rem(d, nz)
    x, c = lax.div(t, 2), lax.rem(t, 2)
    slots = CAP * ny * nz

    def at(dx, core):
        return lax.rem(x + dx, NX) * 2 + core

    t_right, t_left, t_opp, t_sib = at(1, c), at(3, c), at(2, c), at(0, 1 - c)

    def z_peer(i):
        return y * nz + lax.rem(z + i, nz)

    def y_peer(i):
        return lax.rem(y + i, ny) * nz + z

    def remote(src, dst, recv, **where):
        return pltpu.make_async_remote_copy(
            src_ref=src, dst_ref=dst, send_sem=snd, recv_sem=recv,
            device_id=where, device_id_type=MESH,
        )

    def wait_kb(sem, kb):
        part = wv.at[pl.ds(0, kb)]
        remote(part, part, sem, tensor=t_sib).wait_recv()

    own_delta = pltpu.make_async_copy(dl, dlv, lsem.at[0])
    own_og = pltpu.make_async_copy(og, ogf.at[t], lsem.at[1])
    own_tok = pltpu.make_async_copy(tok, tokf.at[pl.ds(t * ROWS, ROWS), :], lsem.at[2])
    own_index = pltpu.make_async_copy(index_in, index, lsem.at[4])
    own_owner = pltpu.make_async_copy(owner_in, owner, lsem.at[5])
    own_owner.start()
    own_index.start()
    own_delta.start()
    own_og.start()
    w_copies = []
    for j in range(4):
        part = pl.ds(j * (D // 4), D // 4)
        w_copies.append(pltpu.make_async_copy(wt.at[part, :], wv.at[part, :], wsem.at[j]))
        w_copies[j].start()
    own_tok.start()

    barrier = pltpu.get_barrier_semaphore()
    along = [{"dp": z_peer(1)}, {"dp": z_peer(nz - 1)}, {"dp": y_peer(1)}, {"dp": y_peer(ny - 1)}]
    near = [{"tensor": t_right}, {"tensor": t_left}, {"tensor": t_sib}] + along
    for where in near:
        pl.semaphore_signal(barrier, inc=1, device_id=where, device_id_type=MESH)

    own_owner.wait()
    owners = [owner[b] for b in range(NB)]
    lane = lax.broadcasted_iota(jnp.int32, (1, HD), 1)
    holds = jnp.full((1, HD), NB, jnp.int32)
    for b in range(NB):
        place = CAP * owners[b]
        for before in range(b):
            place = place + (owners[before] == owners[b]).astype(jnp.int32)
        slot[b] = place
        holds = jnp.where(lane == place, b, holds)
    blkv[...] = holds
    to_smem = pltpu.make_async_copy(blkv, blk, lsem.at[3])
    to_smem.start()

    pl.semaphore_wait(barrier, len(near))

    def tell(i):
        for where in along if i == 0 else along[:2]:
            pl.semaphore_signal(known.at[i], inc=1, device_id=where, device_id_type=MESH)

    def hear(i):
        pl.semaphore_wait(known.at[i], 4 if i == 0 else 2)

    def shard(q, k):
        if q < 2:
            return ogf.at[k, pl.ds(64 * q, 64), :]
        if q < 6:
            return tokf.at[pl.ds(k * ROWS, ROWS), pl.ds(2048 * (q - 2), 2048)]
        return dcp.at[pl.ds(16 * (q - 6), 16), pl.ds(k * ROWS, ROWS), :]

    def mine(q):
        if q < 2:
            return og.at[pl.ds(64 * q, 64), :]
        if q < 6:
            return tok.at[:, pl.ds(2048 * (q - 2), 2048)]
        return shard(q, t)

    def ag(q, kind):
        sib = sbr.at[q // 6]
        if kind == 0:
            return remote(mine(q), shard(q, t), agr.at[q, 0], tensor=t_right)
        if kind == 1:
            return remote(mine(q), shard(q, t), agr.at[q, 1], tensor=t_left)
        if kind == 2:
            return remote(mine(q), shard(q, t), sib, tensor=t_sib)
        if kind == 3:
            return remote(shard(q, t_left), shard(q, t_left), sib, tensor=t_sib)
        if kind == 4:
            return remote(shard(q, t_right), shard(q, t_right), sib, tensor=t_sib)
        if kind == 5 and q % 2 == 0:
            return remote(shard(q, t_left), shard(q, t_left), agr.at[q, 2], tensor=t_right)
        if kind == 5:
            return remote(shard(q, t_right), shard(q, t_right), agr.at[q, 2], tensor=t_left)
        return remote(shard(q, t_opp), shard(q, t_opp), sib, tensor=t_sib)

    def ag_own(q):
        for kind in range(3):
            ag(q, kind).start()

    def ag_pass(q):
        far = q % 2
        ag(q, far).wait_recv()
        ag(q, 5).start()
        ag(q, 3 + far).start()
        ag(q, 1 - far).wait_recv()
        ag(q, 4 - far).start()

    def ag_last(q):
        ag(q, 5).wait_recv()
        ag(q, 6).start()

    def zcopy(i):
        part = dsl.at[pl.ds(CAP * d, CAP)]
        return remote(part, part, dpr.at[0], dp=z_peer(i))

    def ycopy(i):
        part = dsl.at[pl.ds(CAP * nz * y, CAP * nz)]
        return remote(part, part, dpr.at[1], dp=y_peer(i))

    def gycopy(i):
        part = gsl.at[pl.ds(CAP * nz * lax.rem(y + i, ny), CAP * nz)]
        return remote(part, gy.at[i - 1], dpr.at[2], dp=y_peer(i))

    def gzcopy(i):
        part = gys.at[pl.ds(CAP * lax.rem(z + i, nz), CAP)]
        return remote(part, gz.at[i - 1], dpr.at[3], dp=z_peer(i))

    def rs_sib(j):
        return remote(sibs.at[j], sibr.at[j], rsr.at[j, 0], tensor=t_sib)

    def rs_one(j):
        return (
            remote(s1s.at[j, 0], s1r.at[j, 0], rsr.at[j, 1], tensor=t_right),
            remote(s1s.at[j, 1], s1r.at[j, 1], rsr.at[j, 1], tensor=t_left),
        )

    def rs_two(j):
        return (
            remote(s2s.at[j, 0], s2r.at[j, 0], rsr.at[j, 2], tensor=t_right),
            remote(s2s.at[j, 1], s2r.at[j, 1], rsr.at[j, 2], tensor=t_left),
        )

    tell(0)
    for q in range(6):
        ag_own(q)

    own_delta.wait()
    entries = dlv[...].astype(F32)
    for s in range(CAP):
        rows = [entries[s : s + 1, i * HD : (i + 1) * HD] for i in range(ROWS)]
        dsl[CAP * d + s] = jnp.concatenate(rows, axis=0).astype(BF16)
    dcp[NB] = jnp.zeros((HD, HD), BF16)
    gc[NB] = jnp.zeros((ROWS, HD), F32)

    own_og.wait()
    order = [at(dx, core) for core in (c, 1 - c) for dx in (0, 1, 3, 2)]
    for i, k in enumerate(order):
        ogp[pl.ds(i * ROWS, ROWS), :] = ogf[t, pl.ds(pl.multiple_of(k * ROWS, ROWS), ROWS), :]
    hear(0)
    tell(1)

    def backward(i, _):
        rows = pl.ds(pl.multiple_of(i * CW, CW), CW)
        part = lax.dot_general(
            ogp[...], wv[rows, :], (((1,), (1,)), ((), ())), preferred_element_type=F32
        )
        sibs[i] = part[4 * ROWS :].astype(BF16)
        pown[i] = part[: 4 * ROWS]
        rs_sib(i).start()
        return 0

    w_copies[0].wait()
    lax.fori_loop(0, 2, backward, 0)
    hear(1)
    tell(2)
    w_copies[1].wait()
    lax.fori_loop(2, 4, backward, 0)
    hear(2)
    for i in range(1, nz):
        zcopy(i).start()
    ag_pass(0)
    w_copies[2].wait()
    lax.fori_loop(4, 6, backward, 0)
    ag_pass(1)
    w_copies[3].wait()
    lax.fori_loop(6, 8, backward, 0)
    ag_pass(2)
    wait_kb(dpr.at[0], (nz - 1) * KB)
    for i in range(1, ny):
        ycopy(i).start()

    def pair_sum(j, _):
        rs_sib(j).wait_recv()
        total = pown[j] + sibr[j].astype(F32)
        qs[j] = total[:ROWS]
        qr[j] = total[ROWS : 2 * ROWS]
        ql[j] = total[2 * ROWS : 3 * ROWS]
        far = total[3 * ROWS :].astype(BF16)
        s1s[j, 0] = far[:, :HALF]
        s1s[j, 1] = far[:, HALF:]
        return 0

    ag_pass(3)
    lax.fori_loop(0, CHUNKS, pair_sum, 0)
    ag_pass(4)
    ag_pass(5)

    def send_one(j, _):
        for copy in rs_one(j):
            copy.start()
        return 0

    lax.fori_loop(0, CHUNKS, send_one, 0)
    wait_kb(dpr.at[1], (ny - 1) * nz * KB)
    for b in range(NB):
        dcp[b, pl.ds(t * ROWS, ROWS), :] = dsl[slot[b]]
    ag_own(6)
    ag_own(7)
    for q in range(6):
        ag_last(q)
    own_tok.wait()
    own_index.wait()
    wait_kb(sbr.at[0], 6 * 4 * 64)

    for h in range(NT * HEADS_DEV):
        col = h % HEADS_DEV * HD
        og3[h] = ogf[h // HEADS_DEV, :, col : col + HD]
        og16[h] = og3[h, pl.ds(pl.multiple_of(t * ROWS, ROWS), ROWS), :]
    for r in range(D // HD):
        tok3[r] = tokf[:, r * HD : (r + 1) * HD]
    pick_row = lax.broadcasted_iota(jnp.int32, (ROWS, HD), 0) + t * ROWS
    pick = (pick_row == lax.broadcasted_iota(jnp.int32, (ROWS, HD), 1)).astype(BF16)

    def grad_blocks(g, _):
        for i in range(8):
            b = g * 8 + i
            mine_t = lax.dot_general(
                pick, tok3[index[0, b]], (((1,), (1,)), ((), ())), preferred_element_type=F32
            ).astype(BF16)
            gc[b] = jnp.dot(mine_t, og3[index[1, b]], preferred_element_type=F32) * grad_scale
        return 0

    lax.fori_loop(0, NB // 8, grad_blocks, 0)
    to_smem.wait()
    for s in range(slots):
        gsl[s] = gc[blk[0, s]].astype(BF16)
    for i in range(1, ny):
        gycopy(i).start()

    def send_two(j, _):
        part = s1r.at[j]
        remote(part, part, rsr.at[j, 1], tensor=t_sib).wait_recv()
        s2s[j, 0, :, :HALF] = (qr[j, :, :HALF] + s1r[j, 0].astype(F32)).astype(BF16)
        s2s[j, 0, :, HALF:] = qr[j, :, HALF:].astype(BF16)
        s2s[j, 1, :, :HALF] = ql[j, :, :HALF].astype(BF16)
        s2s[j, 1, :, HALF:] = (ql[j, :, HALF:] + s1r[j, 1].astype(F32)).astype(BF16)
        for copy in rs_two(j):
            copy.start()
        return 0

    lax.fori_loop(0, 4, send_two, 0)
    ag_pass(6)
    ag_pass(7)
    lax.fori_loop(4, 8, send_two, 0)

    proj[...] = jnp.zeros_like(proj)

    def forward(i, _):
        rows = pl.ds(pl.multiple_of(i * CW, CW), CW)
        proj[...] += jnp.dot(tokf[:, rows], wv[rows, :], preferred_element_type=F32)
        return 0

    lax.fori_loop(0, 4, forward, 0)

    wait_kb(dpr.at[2], (ny - 1) * nz * KB)
    for s in range(CAP * nz):
        total = gsl[CAP * nz * y + s].astype(F32)
        for i in range(ny - 1):
            total = total + gy[i, s].astype(F32)
        gys[s] = total.astype(BF16)
    for i in range(1, nz):
        gzcopy(i).start()

    lax.fori_loop(4, 8, forward, 0)
    ag_last(6)
    ag_last(7)
    wait_kb(sbr.at[1], 2 * 4 * 64)

    def delta_terms(g, _):
        for i in range(8):
            b = g * 8 + i
            row, head = index[0, b], index[1, b]
            here = slice(i * HD, (i + 1) * HD)
            lhs[:, here] = tok3[row]
            for h in range(HEADS_DEV):
                which = jnp.where(head == t * HEADS_DEV + h, b, NB)
                rhs[here, h * HD : (h + 1) * HD] = dcp[which]
            udel[b] = lax.dot_general(
                og16[head], dcp[b], (((1,), (1,)), ((), ())), preferred_element_type=F32
            )
        proj[...] += jnp.dot(lhs[...], rhs[...], preferred_element_type=F32)
        return 0

    lax.fori_loop(0, NB // 8, delta_terms, 0)

    def last_sum(j, _):
        part = s2r.at[j]
        remote(part, part, rsr.at[j, 2], tensor=t_sib).wait_recv()
        out = qs[j] + s2r[j, 0].astype(F32) + s2r[j, 1].astype(F32)
        igb[:, pl.ds(pl.multiple_of(j * CW, CW), CW)] = out
        return 0

    lax.fori_loop(0, CHUNKS, last_sum, 0)

    wait_kb(dpr.at[3], (nz - 1) * KB)
    for s in range(CAP):
        total = gys[CAP * z + s].astype(F32)
        for i in range(nz - 1):
            total = total + gz[i, s].astype(F32)
        grad_out[s : s + 1, :] = jnp.concatenate([total[i : i + 1] for i in range(ROWS)], axis=1)

    sent = (8 * 7 * 64) + CHUNKS * (128 + 32 + 64) + 2 * (nz - 1) * KB + 2 * (ny - 1) * nz * KB
    part = wv.at[pl.ds(0, sent)]
    remote(part, part, rsr.at[0, 0], tensor=t_sib).wait_send()


def last_kernel(index, igb, udel, proj, grad, dl, m1, m2, proj_out, ig_out, nd, nm1, nm2, total):
    total[...] = igb[...]
    for b in range(NB):
        here = pl.ds(pl.multiple_of(index[0, b] * HD, HD), HD)
        total[:, here] += udel[b]
    ig_out[...] = total[...].astype(BF16)
    proj_out[...] = proj[...].astype(BF16)
    g = grad[...]
    first = 0.9 * m1[...] + 0.1 * g
    second = 0.999 * m2[...] + 0.001 * g * g
    step = 0.02 * (first / CORRECT_ONE) / (jnp.sqrt(second / CORRECT_TWO) + 1e-08)
    nm1[...] = first
    nm2[...] = second
    nd[...] = (dl[...].astype(F32) - step).astype(BF16)


def on_device(ny, nz, tokens, base_weight, out_grad, block_index, block_owner, delta, moment1, moment2):
    slots = CAP * ny * nz
    smem = pl.BlockSpec(memory_space=pltpu.SMEM)
    vmem = pl.BlockSpec(memory_space=pltpu.VMEM)
    hbm = pl.BlockSpec(memory_space=pltpu.HBM)
    index = block_index.T
    dma = pltpu.SemaphoreType.DMA
    grad_scale = 1.0 / math.sqrt(TOK * ny * nz)
    shape = jax.ShapeDtypeStruct

    igb, udel, proj, grad = pl.pallas_call(
        lambda *refs: step_kernel(ny, nz, grad_scale, *refs),
        out_shape=(
            shape((ROWS, D), F32),
            shape((NB, ROWS, HD), F32),
            shape((TOK, WIDTH), F32),
            shape(delta.shape, F32),
        ),
        in_specs=[hbm] * 6,
        out_specs=(vmem,) * 4,
        scratch_shapes=[
            pltpu.VMEM((D, WIDTH), BF16),
            pltpu.VMEM((TOK, D), BF16),
            pltpu.VMEM((D // HD, TOK, HD), BF16),
            pltpu.VMEM((NT, TOK, WIDTH), BF16),
            pltpu.VMEM((NT * HEADS_DEV, TOK, HD), BF16),
            pltpu.VMEM((NT * HEADS_DEV, ROWS, HD), BF16),
            pltpu.VMEM((TOK, WIDTH), BF16),
            pltpu.VMEM(delta.shape, BF16),
            pltpu.VMEM((slots, ROWS, HD), BF16),
            pltpu.VMEM((NB + 1, HD, HD), BF16),
            pltpu.VMEM((NB + 1, ROWS, HD), F32),
            pltpu.VMEM((slots, ROWS, HD), BF16),
            pltpu.VMEM((ny - 1, CAP * nz, ROWS, HD), BF16),
            pltpu.VMEM((CAP * nz, ROWS, HD), BF16),
            pltpu.VMEM((nz - 1, CAP, ROWS, HD), BF16),
            pltpu.VMEM((CHUNKS, 4 * ROWS, CW), F32),
            pltpu.VMEM((CHUNKS, 4 * ROWS, CW), BF16),
            pltpu.VMEM((CHUNKS, 4 * ROWS, CW), BF16),
            pltpu.VMEM((CHUNKS, 2, ROWS, HALF), BF16),
            pltpu.VMEM((CHUNKS, 2, ROWS, HALF), BF16),
            pltpu.VMEM((CHUNKS, 2, ROWS, CW), BF16),
            pltpu.VMEM((CHUNKS, 2, ROWS, CW), BF16),
            pltpu.VMEM((CHUNKS, ROWS, CW), F32),
            pltpu.VMEM((CHUNKS, ROWS, CW), F32),
            pltpu.VMEM((CHUNKS, ROWS, CW), F32),
            pltpu.VMEM((TOK, 8 * HD), BF16),
            pltpu.VMEM((8 * HD, WIDTH), BF16),
            pltpu.VMEM((1, HD), jnp.int32),
            pltpu.SMEM((1, HD), jnp.int32),
            pltpu.SMEM((NB,), jnp.int32),
            pltpu.SMEM((2, NB), jnp.int32),
            pltpu.SMEM((NB,), jnp.int32),
            dma((4,)),
            dma((6,)),
            dma,
            dma((8, 3)),
            dma((2,)),
            dma((4,)),
            dma((CHUNKS, 3)),
            pltpu.SemaphoreType.REGULAR((3,)),
        ],
        compiler_params=pltpu.CompilerParams(
            collective_id=0, has_side_effects=True, vmem_limit_bytes=50 * 1024 * 1024
        ),
        name="step",
    )(*(pltpu.with_memory_space_constraint(a, pltpu.HBM) for a in (index, block_owner, tokens, base_weight, out_grad, delta)))

    return pl.pallas_call(
        last_kernel,
        out_shape=(
            shape((TOK, WIDTH), BF16),
            shape((ROWS, D), BF16),
            shape(delta.shape, BF16),
            shape(delta.shape, F32),
            shape(delta.shape, F32),
        ),
        in_specs=[smem] + [vmem] * 7,
        out_specs=(vmem,) * 5,
        scratch_shapes=[pltpu.VMEM((ROWS, D), F32)],
        compiler_params=pltpu.CompilerParams(vmem_limit_bytes=8 * 1024 * 1024),
        name="last",
    )(index, igb, udel, proj, grad, delta, moment1, moment2)


def solution(mesh):
    dp = mesh.shape["dp"]
    nz = 8
    ny = dp // nz

    def per_device(*args):
        return on_device(ny, nz, *args)

    both = P("dp", "tensor")
    rows = P(("dp", "tensor"), None)
    return jax.shard_map(
        per_device,
        mesh=mesh,
        in_specs=(rows, P(None, "tensor"), both, P(), P(), both, both, both),
        out_specs=(both, rows, both, both, both),
        check_vma=False,
    )
```

```python
import math

import jax
import jax.numpy as jnp
from jax import lax
from jax.experimental import pallas as pl
from jax.experimental.pallas import tpu as pltpu
from jax.sharding import PartitionSpec as P

D = 8192
HD = 128
NB = 32
CAP = 2
NX = 4
NT = 8
ROWS = 16
TOK = 128
WIDTH = 512
HEADS_DEV = 4
CHUNKS = 8
CW = D // CHUNKS
HALF = CW // 2
KB = 8

CORRECT_ONE = 1.0 - 0.9**10
CORRECT_TWO = 1.0 - 0.999**10

F32 = jnp.float32
BF16 = jnp.bfloat16
MESH = pl.DeviceIdType.MESH


def step_kernel(
    ny, nz, grad_scale,
    index_in, owner_in, tok, wt, og, dl,
    igb, udel, proj, grad_out,
    wv, tokf, tok3, tokt, ogf, og3, og16, ogp, dlv, dsl, dcp, gc, gsl, gy, gys, gz,
    pown, sibs, sibr, s1s, s1r, s2s, s2r, qs, qr, ql, lhs, rhs, blkv, blk, slot, index, owner,
    wsem, lsem, snd, agr, sbr, dpr, rsr, known,
):
    d = lax.axis_index("dp")
    t = lax.axis_index("tensor")
    y, z = lax.div(d, nz), lax.rem(d, nz)
    x, c = lax.div(t, 2), lax.rem(t, 2)
    slots = CAP * ny * nz

    def at(dx, core):
        return lax.rem(x + dx, NX) * 2 + core

    t_right, t_left, t_opp, t_sib = at(1, c), at(3, c), at(2, c), at(0, 1 - c)

    def z_peer(i):
        return y * nz + lax.rem(z + i, nz)

    def y_peer(i):
        return lax.rem(y + i, ny) * nz + z

    def remote(src, dst, recv, **where):
        return pltpu.make_async_remote_copy(
            src_ref=src, dst_ref=dst, send_sem=snd, recv_sem=recv,
            device_id=where, device_id_type=MESH,
        )

    def wait_kb(sem, kb):
        part = wv.at[pl.ds(0, kb)]
        remote(part, part, sem, tensor=t_sib).wait_recv()

    own_delta = pltpu.make_async_copy(dl, dlv, lsem.at[0])
    own_og = pltpu.make_async_copy(og, ogf.at[t], lsem.at[1])
    own_tok = pltpu.make_async_copy(tok, tokf.at[pl.ds(t * ROWS, ROWS), :], lsem.at[2])
    own_index = pltpu.make_async_copy(index_in, index, lsem.at[4])
    own_owner = pltpu.make_async_copy(owner_in, owner, lsem.at[5])
    own_owner.start()
    own_index.start()
    own_delta.start()
    own_og.start()
    w_copies = []
    for j in range(4):
        part = pl.ds(j * (D // 4), D // 4)
        w_copies.append(pltpu.make_async_copy(wt.at[part, :], wv.at[part, :], wsem.at[j]))
        w_copies[j].start()
    own_tok.start()

    barrier = pltpu.get_barrier_semaphore()
    along = [{"dp": z_peer(1)}, {"dp": z_peer(nz - 1)}, {"dp": y_peer(1)}, {"dp": y_peer(ny - 1)}]
    near = [{"tensor": t_right}, {"tensor": t_left}, {"tensor": t_sib}] + along
    for where in near:
        pl.semaphore_signal(barrier, inc=1, device_id=where, device_id_type=MESH)

    pl.semaphore_wait(barrier, len(near))

    def tell(i):
        for where in along if i == 0 else along[:2]:
            pl.semaphore_signal(known.at[i], inc=1, device_id=where, device_id_type=MESH)

    def hear(i):
        pl.semaphore_wait(known.at[i], 4 if i == 0 else 2)

    def shard(q, k):
        if q < 2:
            return ogf.at[k, pl.ds(64 * q, 64), :]
        if q < 6:
            return tokf.at[pl.ds(k * ROWS, ROWS), pl.ds(2048 * (q - 2), 2048)]
        return dcp.at[pl.ds(16 * (q - 6), 16), pl.ds(k * ROWS, ROWS), :]

    def mine(q):
        if q < 2:
            return og.at[pl.ds(64 * q, 64), :]
        if q < 6:
            return tok.at[:, pl.ds(2048 * (q - 2), 2048)]
        return shard(q, t)

    def ag(q, kind):
        sib = sbr.at[q]
        if kind == 0:
            return remote(mine(q), shard(q, t), agr.at[q, 0], tensor=t_right)
        if kind == 1:
            return remote(mine(q), shard(q, t), agr.at[q, 1], tensor=t_left)
        if kind == 2:
            return remote(mine(q), shard(q, t), sib, tensor=t_sib)
        if kind == 3:
            return remote(shard(q, t_left), shard(q, t_left), sib, tensor=t_sib)
        if kind == 4:
            return remote(shard(q, t_right), shard(q, t_right), sib, tensor=t_sib)
        if kind == 5 and q % 2 == 0:
            return remote(shard(q, t_left), shard(q, t_left), agr.at[q, 2], tensor=t_right)
        if kind == 5:
            return remote(shard(q, t_right), shard(q, t_right), agr.at[q, 2], tensor=t_left)
        return remote(shard(q, t_opp), shard(q, t_opp), sib, tensor=t_sib)

    def ag_own(q):
        for kind in range(3):
            ag(q, kind).start()

    def ag_pass(q):
        far = q % 2
        ag(q, far).wait_recv()
        ag(q, 5).start()
        ag(q, 3 + far).start()
        ag(q, 1 - far).wait_recv()
        ag(q, 4 - far).start()

    def ag_last(q):
        ag(q, 5).wait_recv()
        ag(q, 6).start()

    def zcopy(i):
        part = dsl.at[pl.ds(CAP * d, CAP)]
        return remote(part, part, dpr.at[0], dp=z_peer(i))

    def ycopy(i):
        part = dsl.at[pl.ds(CAP * nz * y, CAP * nz)]
        return remote(part, part, dpr.at[1], dp=y_peer(i))

    def gycopy(i):
        part = gsl.at[pl.ds(CAP * nz * lax.rem(y + i, ny), CAP * nz)]
        return remote(part, gy.at[i - 1], dpr.at[2], dp=y_peer(i))

    def gzcopy(i):
        part = gys.at[pl.ds(CAP * lax.rem(z + i, nz), CAP)]
        return remote(part, gz.at[i - 1], dpr.at[3], dp=z_peer(i))

    def rs_sib(j):
        return remote(sibs.at[j], sibr.at[j], rsr.at[j, 0], tensor=t_sib)

    def rs_one(j):
        return (
            remote(s1s.at[j, 0], s1r.at[j, 0], rsr.at[j, 1], tensor=t_right),
            remote(s1s.at[j, 1], s1r.at[j, 1], rsr.at[j, 1], tensor=t_left),
        )

    def rs_two(j):
        return (
            remote(s2s.at[j, 0], s2r.at[j, 0], rsr.at[j, 2], tensor=t_right),
            remote(s2s.at[j, 1], s2r.at[j, 1], rsr.at[j, 2], tensor=t_left),
        )

    tell(0)
    for q in range(6):
        ag_own(q)

    own_delta.wait()
    entries = dlv[...].astype(F32)
    for s in range(CAP):
        rows = [entries[s : s + 1, i * HD : (i + 1) * HD] for i in range(ROWS)]
        dsl[CAP * d + s] = jnp.concatenate(rows, axis=0).astype(BF16)
    gc[NB] = jnp.zeros((ROWS, HD), F32)

    own_og.wait()
    order = [at(dx, core) for core in (c, 1 - c) for dx in (0, 1, 3, 2)]
    for i, k in enumerate(order):
        ogp[pl.ds(i * ROWS, ROWS), :] = ogf[t, pl.ds(pl.multiple_of(k * ROWS, ROWS), ROWS), :]
    hear(0)
    tell(1)
    hear(1)
    tell(2)
    hear(2)
    for i in range(1, nz):
        zcopy(i).start()

    def backward(i, _):
        rows = pl.ds(pl.multiple_of(i * CW, CW), CW)
        part = lax.dot_general(
            ogp[...], wv[rows, :], (((1,), (1,)), ((), ())), preferred_element_type=F32
        )
        sibs[i] = part[4 * ROWS :].astype(BF16)
        pown[i] = part[: 4 * ROWS]
        rs_sib(i).start()
        return 0

    for j in range(4):
        ag_pass(j)
        w_copies[j].wait()
        lax.fori_loop(2 * j, 2 * j + 2, backward, 0)
    ag_pass(4)
    wait_kb(dpr.at[0], (nz - 1) * KB)
    for i in range(1, ny):
        ycopy(i).start()

    own_owner.wait()
    owners = [owner[b] for b in range(NB)]
    lane = lax.broadcasted_iota(jnp.int32, (1, HD), 1)
    holds = jnp.full((1, HD), NB, jnp.int32)
    for b in range(NB):
        place = CAP * owners[b]
        for before in range(b):
            place = place + (owners[before] == owners[b]).astype(jnp.int32)
        slot[b] = place
        holds = jnp.where(lane == place, b, holds)
    blkv[...] = holds
    to_smem = pltpu.make_async_copy(blkv, blk, lsem.at[3])
    to_smem.start()

    def pair_sum(j, _):
        rs_sib(j).wait_recv()
        total = pown[j] + sibr[j].astype(F32)
        qs[j] = total[:ROWS]
        qr[j] = total[ROWS : 2 * ROWS]
        ql[j] = total[2 * ROWS : 3 * ROWS]
        far = total[3 * ROWS :].astype(BF16)
        s1s[j, 0] = far[:, :HALF]
        s1s[j, 1] = far[:, HALF:]
        return 0

    ag_pass(5)
    lax.fori_loop(0, CHUNKS, pair_sum, 0)

    def send_one(j, _):
        for copy in rs_one(j):
            copy.start()
        return 0

    lax.fori_loop(0, CHUNKS, send_one, 0)
    own_tok.wait()
    own_index.wait()

    pick_row = lax.broadcasted_iota(jnp.int32, (ROWS, HD), 0) + t * ROWS
    pick = (pick_row == lax.broadcasted_iota(jnp.int32, (ROWS, HD), 1)).astype(BF16)

    def arrange(q):
        wait_kb(sbr.at[q], 4 * 64)
        if q < 2:
            for h in range(NT * HEADS_DEV):
                col = h % HEADS_DEV * HD
                some = slice(64 * q, 64 * q + 64)
                og3[h, some, :] = ogf[h // HEADS_DEV, some, col : col + HD]
                if q == 1:
                    og16[h] = og3[h, pl.ds(pl.multiple_of(t * ROWS, ROWS), ROWS), :]
        else:
            for r in range(16 * (q - 2), 16 * (q - 1)):
                slab = tokf[:, r * HD : (r + 1) * HD]
                tok3[r] = slab
                tokt[r] = lax.dot_general(
                    pick, slab, (((1,), (1,)), ((), ())), preferred_element_type=F32
                ).astype(BF16)

    for q in range(4):
        ag_last(q)
    wait_kb(dpr.at[1], (ny - 1) * nz * KB)
    for b in range(NB):
        dcp[b, pl.ds(t * ROWS, ROWS), :] = dsl[slot[b]]
    ag_own(6)
    ag_own(7)
    arrange(0)
    arrange(1)
    ag_last(4)
    ag_last(5)
    for q in range(2, 6):
        arrange(q)

    for b in range(NB):
        gc[b] = jnp.dot(tokt[index[0, b]], og3[index[1, b]], preferred_element_type=F32) * grad_scale
    to_smem.wait()
    for s in range(slots):
        gsl[s] = gc[blk[0, s]].astype(BF16)
    for i in range(1, ny):
        gycopy(i).start()

    def send_two(j, _):
        part = s1r.at[j]
        remote(part, part, rsr.at[j, 1], tensor=t_sib).wait_recv()
        s2s[j, 0, :, :HALF] = (qr[j, :, :HALF] + s1r[j, 0].astype(F32)).astype(BF16)
        s2s[j, 0, :, HALF:] = qr[j, :, HALF:].astype(BF16)
        s2s[j, 1, :, :HALF] = ql[j, :, :HALF].astype(BF16)
        s2s[j, 1, :, HALF:] = (ql[j, :, HALF:] + s1r[j, 1].astype(F32)).astype(BF16)
        for copy in rs_two(j):
            copy.start()
        return 0

    lax.fori_loop(0, 4, send_two, 0)
    for b in range(NB):
        lhs[:, b * HD : (b + 1) * HD] = tok3[index[0, b]]
    ag_pass(6)
    ag_pass(7)
    lax.fori_loop(4, 8, send_two, 0)

    proj[...] = jnp.zeros_like(proj)

    def forward(i, _):
        rows = pl.ds(pl.multiple_of(i * CW, CW), CW)
        proj[...] += jnp.dot(tokf[:, rows], wv[rows, :], preferred_element_type=F32)
        return 0

    lax.fori_loop(0, CHUNKS, forward, 0)

    wait_kb(dpr.at[2], (ny - 1) * nz * KB)
    for s in range(CAP * nz):
        total = gsl[CAP * nz * y + s].astype(F32)
        for i in range(ny - 1):
            total = total + gy[i, s].astype(F32)
        gys[s] = total.astype(BF16)
    for i in range(1, nz):
        gzcopy(i).start()

    def delta_terms(g, _):
        for i in range(0, 8, 2):
            ends, parts = [], []
            for k in (i, i + 1):
                b = g * 8 + k
                head = index[1, b]
                block = dcp[b]
                for h in range(HEADS_DEV):
                    keep = jnp.where(head == t * HEADS_DEV + h, 1.0, 0.0)
                    keep = jnp.full((1, HD), keep, F32).astype(BF16)
                    rhs[k * HD : (k + 1) * HD, h * HD : (h + 1) * HD] = block * keep
                ends.append(og16[head])
                parts.append(block)
            both = lax.dot_general(
                jnp.concatenate(ends, axis=0), jnp.concatenate(parts, axis=0),
                (((1,), (1,)), ((), ())), preferred_element_type=F32,
            )
            udel[g * 8 + i] = both[:ROWS, :HD]
            udel[g * 8 + i + 1] = both[ROWS:, HD:]
        some = pl.ds(pl.multiple_of(g * 8 * HD, HD), 8 * HD)
        proj[...] += jnp.dot(lhs[:, some], rhs[...], preferred_element_type=F32)
        return 0

    ag_last(6)
    ag_last(7)
    wait_kb(sbr.at[6], 4 * 64)
    lax.fori_loop(0, 2, delta_terms, 0)
    wait_kb(sbr.at[7], 4 * 64)
    lax.fori_loop(2, 4, delta_terms, 0)

    def last_sum(j, _):
        part = s2r.at[j]
        remote(part, part, rsr.at[j, 2], tensor=t_sib).wait_recv()
        out = qs[j] + s2r[j, 0].astype(F32) + s2r[j, 1].astype(F32)
        igb[:, pl.ds(pl.multiple_of(j * CW, CW), CW)] = out
        return 0

    lax.fori_loop(0, CHUNKS, last_sum, 0)

    wait_kb(dpr.at[3], (nz - 1) * KB)
    for s in range(CAP):
        total = gys[CAP * z + s].astype(F32)
        for i in range(nz - 1):
            total = total + gz[i, s].astype(F32)
        grad_out[s : s + 1, :] = jnp.concatenate([total[i : i + 1] for i in range(ROWS)], axis=1)

    sent = (8 * 7 * 64) + CHUNKS * (128 + 32 + 64) + 2 * (nz - 1) * KB + 2 * (ny - 1) * nz * KB
    part = wv.at[pl.ds(0, sent)]
    remote(part, part, rsr.at[0, 0], tensor=t_sib).wait_send()


def last_kernel(index, igb, udel, proj, grad, dl, m1, m2, proj_out, ig_out, nd, nm1, nm2, total):
    total[...] = igb[...]
    for b in range(NB):
        here = pl.ds(pl.multiple_of(index[0, b] * HD, HD), HD)
        total[:, here] += udel[b]
    ig_out[...] = total[...].astype(BF16)
    proj_out[...] = proj[...].astype(BF16)
    g = grad[...]
    first = 0.9 * m1[...] + 0.1 * g
    second = 0.999 * m2[...] + 0.001 * g * g
    step = 0.02 * (first / CORRECT_ONE) / (jnp.sqrt(second / CORRECT_TWO) + 1e-08)
    nm1[...] = first
    nm2[...] = second
    nd[...] = (dl[...].astype(F32) - step).astype(BF16)


def on_device(ny, nz, tokens, base_weight, out_grad, block_index, block_owner, delta, moment1, moment2):
    slots = CAP * ny * nz
    smem = pl.BlockSpec(memory_space=pltpu.SMEM)
    vmem = pl.BlockSpec(memory_space=pltpu.VMEM)
    hbm = pl.BlockSpec(memory_space=pltpu.HBM)
    index = block_index.T
    dma = pltpu.SemaphoreType.DMA
    grad_scale = 1.0 / math.sqrt(TOK * ny * nz)
    shape = jax.ShapeDtypeStruct

    igb, udel, proj, grad = pl.pallas_call(
        lambda *refs: step_kernel(ny, nz, grad_scale, *refs),
        out_shape=(
            shape((ROWS, D), F32),
            shape((NB, ROWS, HD), F32),
            shape((TOK, WIDTH), F32),
            shape(delta.shape, F32),
        ),
        in_specs=[hbm] * 6,
        out_specs=(vmem,) * 4,
        scratch_shapes=[
            pltpu.VMEM((D, WIDTH), BF16),
            pltpu.VMEM((TOK, D), BF16),
            pltpu.VMEM((D // HD, TOK, HD), BF16),
            pltpu.VMEM((D // HD, ROWS, HD), BF16),
            pltpu.VMEM((NT, TOK, WIDTH), BF16),
            pltpu.VMEM((NT * HEADS_DEV, TOK, HD), BF16),
            pltpu.VMEM((NT * HEADS_DEV, ROWS, HD), BF16),
            pltpu.VMEM((TOK, WIDTH), BF16),
            pltpu.VMEM(delta.shape, BF16),
            pltpu.VMEM((slots, ROWS, HD), BF16),
            pltpu.VMEM((NB, HD, HD), BF16),
            pltpu.VMEM((NB + 1, ROWS, HD), F32),
            pltpu.VMEM((slots, ROWS, HD), BF16),
            pltpu.VMEM((ny - 1, CAP * nz, ROWS, HD), BF16),
            pltpu.VMEM((CAP * nz, ROWS, HD), BF16),
            pltpu.VMEM((nz - 1, CAP, ROWS, HD), BF16),
            pltpu.VMEM((CHUNKS, 4 * ROWS, CW), F32),
            pltpu.VMEM((CHUNKS, 4 * ROWS, CW), BF16),
            pltpu.VMEM((CHUNKS, 4 * ROWS, CW), BF16),
            pltpu.VMEM((CHUNKS, 2, ROWS, HALF), BF16),
            pltpu.VMEM((CHUNKS, 2, ROWS, HALF), BF16),
            pltpu.VMEM((CHUNKS, 2, ROWS, CW), BF16),
            pltpu.VMEM((CHUNKS, 2, ROWS, CW), BF16),
            pltpu.VMEM((CHUNKS, ROWS, CW), F32),
            pltpu.VMEM((CHUNKS, ROWS, CW), F32),
            pltpu.VMEM((CHUNKS, ROWS, CW), F32),
            pltpu.VMEM((TOK, NB * HD), BF16),
            pltpu.VMEM((8 * HD, WIDTH), BF16),
            pltpu.VMEM((1, HD), jnp.int32),
            pltpu.SMEM((1, HD), jnp.int32),
            pltpu.SMEM((NB,), jnp.int32),
            pltpu.SMEM((2, NB), jnp.int32),
            pltpu.SMEM((NB,), jnp.int32),
            dma((4,)),
            dma((6,)),
            dma,
            dma((8, 3)),
            dma((8,)),
            dma((4,)),
            dma((CHUNKS, 3)),
            pltpu.SemaphoreType.REGULAR((3,)),
        ],
        compiler_params=pltpu.CompilerParams(
            collective_id=0, has_side_effects=True, vmem_limit_bytes=50 * 1024 * 1024
        ),
        name="step",
    )(*(pltpu.with_memory_space_constraint(a, pltpu.HBM) for a in (index, block_owner, tokens, base_weight, out_grad, delta)))

    return pl.pallas_call(
        last_kernel,
        out_shape=(
            shape((TOK, WIDTH), BF16),
            shape((ROWS, D), BF16),
            shape(delta.shape, BF16),
            shape(delta.shape, F32),
            shape(delta.shape, F32),
        ),
        in_specs=[smem] + [vmem] * 7,
        out_specs=(vmem,) * 5,
        scratch_shapes=[pltpu.VMEM((ROWS, D), F32)],
        compiler_params=pltpu.CompilerParams(vmem_limit_bytes=8 * 1024 * 1024),
        name="last",
    )(index, igb, udel, proj, grad, delta, moment1, moment2)


def solution(mesh):
    dp = mesh.shape["dp"]
    nz = 8
    ny = dp // nz

    def per_device(*args):
        return on_device(ny, nz, *args)

    both = P("dp", "tensor")
    rows = P(("dp", "tensor"), None)
    return jax.shard_map(
        per_device,
        mesh=mesh,
        in_specs=(rows, P(None, "tensor"), both, P(), P(), both, both, both),
        out_specs=(both, rows, both, both, both),
        check_vma=False,
    )
```

```python
import math

import jax
import jax.numpy as jnp
from jax import lax
from jax.experimental import pallas as pl
from jax.experimental.pallas import tpu as pltpu
from jax.sharding import PartitionSpec as P

D = 8192
HD = 128
NB = 32
CAP = 2
NX = 4
NT = 8
ROWS = 16
TOK = 128
WIDTH = 512
HEADS_DEV = 4
CHUNKS = 8
CW = D // CHUNKS
HALF = CW // 2
KB = 8

CORRECT_ONE = 1.0 - 0.9**10
CORRECT_TWO = 1.0 - 0.999**10

F32 = jnp.float32
BF16 = jnp.bfloat16
MESH = pl.DeviceIdType.MESH


def step_kernel(
    ny, nz, grad_scale,
    index_in, owner_in, tok, wt, og, dl,
    igb, udel, proj, grad_out,
    wv, tokf, tok3, tokt, ogf, og3, og16, ogp, dlv, dsl, dcp, gc, gsl, gy, gys, gz,
    pown, sibs, sibr, s1s, s1r, s2s, s2r, qs, qr, ql, lhs, rhs, blkv, blk, slot, index, owner,
    wsem, lsem, snd, agr, sbr, dpr, rsr, known,
):
    d = lax.axis_index("dp")
    t = lax.axis_index("tensor")
    y, z = lax.div(d, nz), lax.rem(d, nz)
    x, c = lax.div(t, 2), lax.rem(t, 2)

    def at(dx, core):
        return lax.rem(x + dx, NX) * 2 + core

    t_right, t_left, t_opp, t_sib = at(1, c), at(3, c), at(2, c), at(0, 1 - c)

    def z_peer(i):
        return y * nz + lax.rem(z + i, nz)

    def y_peer(i):
        return lax.rem(y + i, ny) * nz + z

    def remote(src, dst, recv, **where):
        return pltpu.make_async_remote_copy(
            src_ref=src, dst_ref=dst, send_sem=snd, recv_sem=recv,
            device_id=where, device_id_type=MESH,
        )

    def wait_kb(sem, kb):
        part = wv.at[pl.ds(0, kb)]
        remote(part, part, sem, tensor=t_sib).wait_recv()

    own_delta = pltpu.make_async_copy(dl, dlv, lsem.at[0])
    own_og = pltpu.make_async_copy(og, ogf.at[t], lsem.at[1])
    own_tok = pltpu.make_async_copy(tok, tokf.at[pl.ds(t * ROWS, ROWS), :], lsem.at[2])
    own_index = pltpu.make_async_copy(index_in, index, lsem.at[4])
    own_owner = pltpu.make_async_copy(owner_in, owner, lsem.at[5])
    own_owner.start()
    own_index.start()
    own_delta.start()
    own_og.start()
    w_copies = []
    for j in range(4):
        part = pl.ds(j * (D // 4), D // 4)
        w_copies.append(pltpu.make_async_copy(wt.at[part, :], wv.at[part, :], wsem.at[j]))
        w_copies[j].start()
    own_tok.start()

    barrier = pltpu.get_barrier_semaphore()
    along = [{"dp": z_peer(2)}, {"dp": z_peer(nz - 2)}, {"dp": y_peer(1)}, {"dp": y_peer(ny - 1)}]
    near = [{"tensor": t_right}, {"tensor": t_left}, {"tensor": t_sib}] + along
    near += [{"dp": z_peer(1)}, {"dp": z_peer(nz - 1)}]
    for where in near:
        pl.semaphore_signal(barrier, inc=1, device_id=where, device_id_type=MESH)

    pl.semaphore_wait(barrier, len(near))

    def tell():
        for where in along:
            pl.semaphore_signal(known, inc=1, device_id=where, device_id_type=MESH)

    def shard(q, k):
        if q < 2:
            return ogf.at[k, pl.ds(64 * q, 64), :]
        if q < 6:
            return tokf.at[pl.ds(k * ROWS, ROWS), pl.ds(2048 * (q - 2), 2048)]
        return dcp.at[pl.ds(16 * (q - 6), 16), pl.ds(k * ROWS, ROWS), :]

    def mine(q):
        if q < 2:
            return og.at[pl.ds(64 * q, 64), :]
        if q < 6:
            return tok.at[:, pl.ds(2048 * (q - 2), 2048)]
        return shard(q, t)

    def ag(q, kind):
        sib = sbr.at[q]
        if kind == 0:
            return remote(mine(q), shard(q, t), agr.at[q, 0], tensor=t_right)
        if kind == 1:
            return remote(mine(q), shard(q, t), agr.at[q, 1], tensor=t_left)
        if kind == 2:
            return remote(mine(q), shard(q, t), sib, tensor=t_sib)
        if kind == 3:
            return remote(shard(q, t_left), shard(q, t_left), sib, tensor=t_sib)
        if kind == 4:
            return remote(shard(q, t_right), shard(q, t_right), sib, tensor=t_sib)
        if kind == 5 and q % 2 == 0:
            return remote(shard(q, t_left), shard(q, t_left), agr.at[q, 2], tensor=t_right)
        if kind == 5:
            return remote(shard(q, t_right), shard(q, t_right), agr.at[q, 2], tensor=t_left)
        return remote(shard(q, t_opp), shard(q, t_opp), sib, tensor=t_sib)

    def ag_own(q):
        for kind in range(3):
            ag(q, kind).start()

    def ag_pass(q):
        far = q % 2
        ag(q, far).wait_recv()
        ag(q, 5).start()
        ag(q, 3 + far).start()
        ag(q, 1 - far).wait_recv()
        ag(q, 4 - far).start()

    def ag_last(q):
        ag(q, 5).wait_recv()
        ag(q, 6).start()

    def zcopy(i):
        part = dsl.at[pl.ds(CAP * d, CAP)]
        return remote(part, part, dpr.at[0], dp=z_peer(i))

    def ycopy(i):
        part = dsl.at[pl.ds(CAP * nz * y, CAP * nz)]
        return remote(part, part, dpr.at[1], dp=y_peer(i))

    z_order = sorted(range(nz), key=lambda o: -min(o, nz - o))
    part_slots = CAP * nz // 2

    def gycopy(i, part):
        some = pl.ds(part * part_slots, part_slots)
        return remote(gsl.at[i, some], gy.at[i - 1, some], dpr.at[2 + part], dp=y_peer(i))

    def gzcopy(p):
        return remote(gys.at[pl.ds(CAP * p, CAP)], gz.at[p], dpr.at[4], dp=z_peer(z_order[p]))

    def rs_sib(j):
        return remote(sibs.at[j], sibr.at[j], rsr.at[0], tensor=t_sib)

    def rs_one(j):
        return (
            remote(s1s.at[j, 0], s1r.at[j, 0], rsr.at[1 + lax.div(j, 4)], tensor=t_right),
            remote(s1s.at[j, 1], s1r.at[j, 1], rsr.at[1 + lax.div(j, 4)], tensor=t_left),
        )

    def rs_two(j):
        return (
            remote(s2s.at[j, 0], s2r.at[j, 0], rsr.at[3], tensor=t_right),
            remote(s2s.at[j, 1], s2r.at[j, 1], rsr.at[3], tensor=t_left),
        )

    tell()
    for q in range(6):
        ag_own(q)

    own_delta.wait()
    entries = dlv[...].astype(F32)
    for s in range(CAP):
        rows = [entries[s : s + 1, i * HD : (i + 1) * HD] for i in range(ROWS)]
        dsl[CAP * d + s] = jnp.concatenate(rows, axis=0).astype(BF16)
    gc[NB] = jnp.zeros((ROWS, HD), F32)

    own_og.wait()
    order = [at(dx, core) for core in (c, 1 - c) for dx in (0, 1, 3, 2)]
    for i, k in enumerate(order):
        ogp[pl.ds(i * ROWS, ROWS), :] = ogf[t, pl.ds(pl.multiple_of(k * ROWS, ROWS), ROWS), :]
    pl.semaphore_wait(known, len(along))
    for i in range(1, nz):
        zcopy(i).start()

    def backward(i, _):
        rows = pl.ds(pl.multiple_of(i * CW, CW), CW)
        part = lax.dot_general(
            ogp[...], wv[rows, :], (((1,), (1,)), ((), ())), preferred_element_type=F32
        )
        sibs[i] = part[4 * ROWS :].astype(BF16)
        pown[i] = part[: 4 * ROWS]
        rs_sib(i).start()
        return 0

    for j in range(4):
        w_copies[j].wait()
        lax.fori_loop(2 * j, 2 * j + 2, backward, 0)
        ag_pass(j)
        if j == 2:
            wait_kb(dpr.at[0], (nz - 1) * KB)
            for i in range(1, ny):
                ycopy(i).start()

    own_owner.wait()
    owners = [owner[b] for b in range(NB)]
    lane = lax.broadcasted_iota(jnp.int32, (1, HD), 1)
    holds = jnp.full((1, HD), NB, jnp.int32)
    for b in range(NB):
        place = CAP * owners[b]
        for before in range(b):
            place = place + (owners[before] == owners[b]).astype(jnp.int32)
        slot[b] = place
        holds = jnp.where(lane == place, b, holds)
    blkv[...] = holds
    to_smem = pltpu.make_async_copy(blkv, blk, lsem.at[3])
    to_smem.start()

    def pair_sum(j, _):
        total = pown[j] + sibr[j].astype(F32)
        qs[j] = total[:ROWS]
        qr[j] = total[ROWS : 2 * ROWS]
        ql[j] = total[2 * ROWS : 3 * ROWS]
        far = total[3 * ROWS :].astype(BF16)
        s1s[j, 0] = far[:, :HALF]
        s1s[j, 1] = far[:, HALF:]
        return 0

    ag_pass(4)
    ag_pass(5)
    wait_kb(rsr.at[0], CHUNKS * 128)
    lax.fori_loop(0, CHUNKS, pair_sum, 0)

    def send_one(j, _):
        for copy in rs_one(j):
            copy.start()
        return 0

    lax.fori_loop(0, CHUNKS, send_one, 0)
    wait_kb(dpr.at[1], (ny - 1) * nz * KB)
    for b in range(NB):
        dcp[b, pl.ds(t * ROWS, ROWS), :] = dsl[slot[b]]
    ag_own(6)
    ag_own(7)
    own_tok.wait()
    own_index.wait()

    pick_row = lax.broadcasted_iota(jnp.int32, (ROWS, HD), 0) + t * ROWS
    pick = (pick_row == lax.broadcasted_iota(jnp.int32, (ROWS, HD), 1)).astype(BF16)

    def arrange(q):
        wait_kb(sbr.at[q], 4 * 64)
        if q < 2:
            for h in range(NT * HEADS_DEV):
                col = h % HEADS_DEV * HD
                some = slice(64 * q, 64 * q + 64)
                og3[h, some, :] = ogf[h // HEADS_DEV, some, col : col + HD]
                if q == 1:
                    og16[h] = og3[h, pl.ds(pl.multiple_of(t * ROWS, ROWS), ROWS), :]
        else:
            for r in range(16 * (q - 2), 16 * (q - 1)):
                slab = tokf[:, r * HD : (r + 1) * HD]
                tok3[r] = slab
                tokt[r] = lax.dot_general(
                    pick, slab, (((1,), (1,)), ((), ())), preferred_element_type=F32
                ).astype(BF16)

    ag_last(0)
    ag_last(1)
    ag_last(2)
    ag_last(3)
    arrange(0)
    arrange(1)
    ag_last(4)
    ag_last(5)
    for q in range(2, 6):
        arrange(q)

    for b in range(NB):
        gc[b] = jnp.dot(tokt[index[0, b]], og3[index[1, b]], preferred_element_type=F32) * grad_scale
    to_smem.wait()
    for i in range(ny):
        for p, o in enumerate(z_order):
            for s in range(CAP):
                place = CAP * (y_peer(i) - z + lax.rem(z + o, nz)) + s
                gsl[i, CAP * p + s] = gc[blk[0, place]].astype(BF16)
    for part in range(2):
        for i in range(1, ny):
            gycopy(i, part).start()

    def send_two(j, _):
        s2s[j, 0, :, :HALF] = (qr[j, :, :HALF] + s1r[j, 0].astype(F32)).astype(BF16)
        s2s[j, 0, :, HALF:] = qr[j, :, HALF:].astype(BF16)
        s2s[j, 1, :, :HALF] = ql[j, :, :HALF].astype(BF16)
        s2s[j, 1, :, HALF:] = (ql[j, :, HALF:] + s1r[j, 1].astype(F32)).astype(BF16)
        for copy in rs_two(j):
            copy.start()
        return 0

    for b in range(NB):
        lhs[:, b * HD : (b + 1) * HD] = tok3[index[0, b]]
    ag_pass(6)
    ag_pass(7)
    for half in range(2):
        wait_kb(rsr.at[1 + half], 128)
        lax.fori_loop(4 * half, 4 * half + 4, send_two, 0)

    proj[...] = jnp.zeros_like(proj)

    def forward(i, _):
        rows = pl.ds(pl.multiple_of(i * CW, CW), CW)
        proj[...] += jnp.dot(tokf[:, rows], wv[rows, :], preferred_element_type=F32)
        return 0

    lax.fori_loop(0, CHUNKS, forward, 0)

    def delta_terms(g, _):
        for i in range(0, 8, 2):
            ends, parts = [], []
            for k in (i, i + 1):
                b = g * 8 + k
                head = index[1, b]
                block = dcp[b]
                for h in range(HEADS_DEV):
                    keep = jnp.where(head == t * HEADS_DEV + h, 1.0, 0.0)
                    keep = jnp.full((1, HD), keep, F32).astype(BF16)
                    rhs[k * HD : (k + 1) * HD, h * HD : (h + 1) * HD] = block * keep
                ends.append(og16[head])
                parts.append(block)
            both = lax.dot_general(
                jnp.concatenate(ends, axis=0), jnp.concatenate(parts, axis=0),
                (((1,), (1,)), ((), ())), preferred_element_type=F32,
            )
            udel[g * 8 + i] = both[:ROWS, :HD]
            udel[g * 8 + i + 1] = both[ROWS:, HD:]
        some = pl.ds(pl.multiple_of(g * 8 * HD, HD), 8 * HD)
        proj[...] += jnp.dot(lhs[:, some], rhs[...], preferred_element_type=F32)
        return 0

    ag_last(6)
    ag_last(7)
    for part in range(2):
        wait_kb(dpr.at[2 + part], (ny - 1) * nz * KB // 2)
        for p in range(part * nz // 2, (part + 1) * nz // 2):
            for s in range(CAP * p, CAP * (p + 1)):
                total = gsl[0, s].astype(F32)
                for i in range(ny - 1):
                    total = total + gy[i, s].astype(F32)
                gys[s] = total.astype(BF16)
        for p in range(part * nz // 2, (part + 1) * nz // 2):
            if p < nz - 1:
                gzcopy(p).start()

    wait_kb(sbr.at[6], 4 * 64)
    lax.fori_loop(0, 2, delta_terms, 0)
    wait_kb(sbr.at[7], 4 * 64)
    lax.fori_loop(2, 4, delta_terms, 0)

    def last_sum(j, _):
        out = qs[j] + s2r[j, 0].astype(F32) + s2r[j, 1].astype(F32)
        igb[:, pl.ds(pl.multiple_of(j * CW, CW), CW)] = out
        return 0

    wait_kb(rsr.at[3], CHUNKS * 64)
    lax.fori_loop(0, CHUNKS, last_sum, 0)

    wait_kb(dpr.at[4], (nz - 1) * KB)
    for s in range(CAP):
        total = gys[CAP * (nz - 1) + s].astype(F32)
        for i in range(nz - 1):
            total = total + gz[i, s].astype(F32)
        grad_out[s : s + 1, :] = jnp.concatenate([total[i : i + 1] for i in range(ROWS)], axis=1)

    sent = (8 * 7 * 64) + CHUNKS * (128 + 32 + 64) + 2 * (nz - 1) * KB + 2 * (ny - 1) * nz * KB
    part = wv.at[pl.ds(0, sent)]
    remote(part, part, rsr.at[0], tensor=t_sib).wait_send()


def last_kernel(index, igb, udel, proj, grad, dl, m1, m2, proj_out, ig_out, nd, nm1, nm2, total):
    total[...] = igb[...]
    for b in range(NB):
        here = pl.ds(pl.multiple_of(index[0, b] * HD, HD), HD)
        total[:, here] += udel[b]
    ig_out[...] = total[...].astype(BF16)
    proj_out[...] = proj[...].astype(BF16)
    g = grad[...]
    first = 0.9 * m1[...] + 0.1 * g
    second = 0.999 * m2[...] + 0.001 * g * g
    step = 0.02 * (first / CORRECT_ONE) / (jnp.sqrt(second / CORRECT_TWO) + 1e-08)
    nm1[...] = first
    nm2[...] = second
    nd[...] = (dl[...].astype(F32) - step).astype(BF16)


def on_device(ny, nz, tokens, base_weight, out_grad, block_index, block_owner, delta, moment1, moment2):
    slots = CAP * ny * nz
    smem = pl.BlockSpec(memory_space=pltpu.SMEM)
    vmem = pl.BlockSpec(memory_space=pltpu.VMEM)
    hbm = pl.BlockSpec(memory_space=pltpu.HBM)
    index = block_index.T
    dma = pltpu.SemaphoreType.DMA
    grad_scale = 1.0 / math.sqrt(TOK * ny * nz)
    shape = jax.ShapeDtypeStruct

    igb, udel, proj, grad = pl.pallas_call(
        lambda *refs: step_kernel(ny, nz, grad_scale, *refs),
        out_shape=(
            shape((ROWS, D), F32),
            shape((NB, ROWS, HD), F32),
            shape((TOK, WIDTH), F32),
            shape(delta.shape, F32),
        ),
        in_specs=[hbm] * 6,
        out_specs=(vmem,) * 4,
        scratch_shapes=[
            pltpu.VMEM((D, WIDTH), BF16),
            pltpu.VMEM((TOK, D), BF16),
            pltpu.VMEM((D // HD, TOK, HD), BF16),
            pltpu.VMEM((D // HD, ROWS, HD), BF16),
            pltpu.VMEM((NT, TOK, WIDTH), BF16),
            pltpu.VMEM((NT * HEADS_DEV, TOK, HD), BF16),
            pltpu.VMEM((NT * HEADS_DEV, ROWS, HD), BF16),
            pltpu.VMEM((TOK, WIDTH), BF16),
            pltpu.VMEM(delta.shape, BF16),
            pltpu.VMEM((slots, ROWS, HD), BF16),
            pltpu.VMEM((NB, HD, HD), BF16),
            pltpu.VMEM((NB + 1, ROWS, HD), F32),
            pltpu.VMEM((ny, CAP * nz, ROWS, HD), BF16),
            pltpu.VMEM((ny - 1, CAP * nz, ROWS, HD), BF16),
            pltpu.VMEM((CAP * nz, ROWS, HD), BF16),
            pltpu.VMEM((nz - 1, CAP, ROWS, HD), BF16),
            pltpu.VMEM((CHUNKS, 4 * ROWS, CW), F32),
            pltpu.VMEM((CHUNKS, 4 * ROWS, CW), BF16),
            pltpu.VMEM((CHUNKS, 4 * ROWS, CW), BF16),
            pltpu.VMEM((CHUNKS, 2, ROWS, HALF), BF16),
            pltpu.VMEM((CHUNKS, 2, ROWS, HALF), BF16),
            pltpu.VMEM((CHUNKS, 2, ROWS, CW), BF16),
            pltpu.VMEM((CHUNKS, 2, ROWS, CW), BF16),
            pltpu.VMEM((CHUNKS, ROWS, CW), F32),
            pltpu.VMEM((CHUNKS, ROWS, CW), F32),
            pltpu.VMEM((CHUNKS, ROWS, CW), F32),
            pltpu.VMEM((TOK, NB * HD), BF16),
            pltpu.VMEM((8 * HD, WIDTH), BF16),
            pltpu.VMEM((1, HD), jnp.int32),
            pltpu.SMEM((1, HD), jnp.int32),
            pltpu.SMEM((NB,), jnp.int32),
            pltpu.SMEM((2, NB), jnp.int32),
            pltpu.SMEM((NB,), jnp.int32),
            dma((4,)),
            dma((6,)),
            dma,
            dma((8, 3)),
            dma((8,)),
            dma((5,)),
            dma((4,)),
            pltpu.SemaphoreType.REGULAR,
        ],
        compiler_params=pltpu.CompilerParams(
            collective_id=0, has_side_effects=True, vmem_limit_bytes=50 * 1024 * 1024
        ),
        name="step",
    )(*(pltpu.with_memory_space_constraint(a, pltpu.HBM) for a in (index, block_owner, tokens, base_weight, out_grad, delta)))

    return pl.pallas_call(
        last_kernel,
        out_shape=(
            shape((TOK, WIDTH), BF16),
            shape((ROWS, D), BF16),
            shape(delta.shape, BF16),
            shape(delta.shape, F32),
            shape(delta.shape, F32),
        ),
        in_specs=[smem] + [vmem] * 7,
        out_specs=(vmem,) * 5,
        scratch_shapes=[pltpu.VMEM((ROWS, D), F32)],
        compiler_params=pltpu.CompilerParams(vmem_limit_bytes=8 * 1024 * 1024),
        name="last",
    )(index, igb, udel, proj, grad, delta, moment1, moment2)


def solution(mesh):
    dp = mesh.shape["dp"]
    nz = 8
    ny = dp // nz

    def per_device(*args):
        return on_device(ny, nz, *args)

    both = P("dp", "tensor")
    rows = P(("dp", "tensor"), None)
    return jax.shard_map(
        per_device,
        mesh=mesh,
        in_specs=(rows, P(None, "tensor"), both, P(), P(), both, both, both),
        out_specs=(both, rows, both, both, both),
        check_vma=False,
    )
```

```python
import math

import jax
import jax.numpy as jnp
from jax import lax
from jax.experimental import pallas as pl
from jax.experimental.pallas import tpu as pltpu
from jax.sharding import PartitionSpec as P

D = 8192
HD = 128
NB = 32
CAP = 2
NX = 4
NT = 8
ROWS = 16
TOK = 128
WIDTH = 512
HEADS_DEV = 4
CHUNKS = 8
CW = D // CHUNKS
HALF = CW // 2
KB = 8

CORRECT_ONE = 1.0 - 0.9**10
CORRECT_TWO = 1.0 - 0.999**10

F32 = jnp.float32
BF16 = jnp.bfloat16
MESH = pl.DeviceIdType.MESH


def step_kernel(
    ny, nz, grad_scale,
    index_in, owner_in, tok, wt, og, dl,
    igb, udel, proj, grad_out,
    wv, tokf, tok3, tokt, ogf, og3, og16, ogp, dlv, dsl, dcp, gc, gsl, gy, gys, gz,
    pown, sibs, sibr, s1s, s1r, s2s, s2r, qs, qr, ql, lhs, rhs, blkv, blk, slot, index, owner,
    wsem, lsem, snd, agr, sbr, dpr, rsr, known,
):
    d = lax.axis_index("dp")
    t = lax.axis_index("tensor")
    y, z = lax.div(d, nz), lax.rem(d, nz)
    x, c = lax.div(t, 2), lax.rem(t, 2)

    def at(dx, core):
        return lax.rem(x + dx, NX) * 2 + core

    t_right, t_left, t_opp, t_sib = at(1, c), at(3, c), at(2, c), at(0, 1 - c)

    def z_peer(i):
        return y * nz + lax.rem(z + i, nz)

    def y_peer(i):
        return lax.rem(y + i, ny) * nz + z

    def remote(src, dst, recv, **where):
        return pltpu.make_async_remote_copy(
            src_ref=src, dst_ref=dst, send_sem=snd, recv_sem=recv,
            device_id=where, device_id_type=MESH,
        )

    def wait_kb(sem, kb):
        part = wv.at[pl.ds(0, kb)]
        remote(part, part, sem, tensor=t_sib).wait_recv()

    own_delta = pltpu.make_async_copy(dl, dlv, lsem.at[0])
    own_og = pltpu.make_async_copy(og, ogf.at[t], lsem.at[1])
    own_tok = pltpu.make_async_copy(tok, tokf.at[pl.ds(t * ROWS, ROWS), :], lsem.at[2])
    own_index = pltpu.make_async_copy(index_in, index, lsem.at[4])
    own_owner = pltpu.make_async_copy(owner_in, owner, lsem.at[5])
    own_owner.start()
    own_index.start()
    own_delta.start()
    own_og.start()
    w_copies = []
    for j in range(4):
        part = pl.ds(j * (D // 4), D // 4)
        w_copies.append(pltpu.make_async_copy(wt.at[part, :], wv.at[part, :], wsem.at[j]))
        w_copies[j].start()
    own_tok.start()

    barrier = pltpu.get_barrier_semaphore()
    along = [{"dp": z_peer(2)}, {"dp": z_peer(nz - 2)}, {"dp": y_peer(1)}, {"dp": y_peer(ny - 1)}]
    near = [{"tensor": t_right}, {"tensor": t_left}, {"tensor": t_sib}] + along
    near += [{"dp": z_peer(1)}, {"dp": z_peer(nz - 1)}]
    for where in near:
        pl.semaphore_signal(barrier, inc=1, device_id=where, device_id_type=MESH)

    pl.semaphore_wait(barrier, len(near))

    def tell():
        for where in along:
            pl.semaphore_signal(known, inc=1, device_id=where, device_id_type=MESH)

    def shard(q, k):
        if q < 2:
            return ogf.at[k, pl.ds(64 * q, 64), :]
        if q < 6:
            return tokf.at[pl.ds(k * ROWS, ROWS), pl.ds(2048 * (q - 2), 2048)]
        return dcp.at[pl.ds(16 * (q - 6), 16), pl.ds(k * ROWS, ROWS), :]

    def mine(q):
        if q < 2:
            return og.at[pl.ds(64 * q, 64), :]
        if q < 6:
            return tok.at[:, pl.ds(2048 * (q - 2), 2048)]
        return shard(q, t)

    def ag(q, kind):
        sib = sbr.at[q]
        if kind == 0:
            return remote(mine(q), shard(q, t), agr.at[q, 0], tensor=t_right)
        if kind == 1:
            return remote(mine(q), shard(q, t), agr.at[q, 1], tensor=t_left)
        if kind == 2:
            return remote(mine(q), shard(q, t), sib, tensor=t_sib)
        if kind == 3:
            return remote(shard(q, t_left), shard(q, t_left), sib, tensor=t_sib)
        if kind == 4:
            return remote(shard(q, t_right), shard(q, t_right), sib, tensor=t_sib)
        if kind == 5 and q % 2 == 0:
            return remote(shard(q, t_left), shard(q, t_left), agr.at[q, 2], tensor=t_right)
        if kind == 5:
            return remote(shard(q, t_right), shard(q, t_right), agr.at[q, 2], tensor=t_left)
        return remote(shard(q, t_opp), shard(q, t_opp), sib, tensor=t_sib)

    def ag_own(q):
        for kind in range(3):
            ag(q, kind).start()

    def ag_pass(q):
        far = q % 2
        ag(q, far).wait_recv()
        ag(q, 5).start()
        ag(q, 3 + far).start()
        ag(q, 1 - far).wait_recv()
        ag(q, 4 - far).start()

    def ag_last(q):
        ag(q, 5).wait_recv()
        ag(q, 6).start()

    def zcopy(i):
        part = dsl.at[pl.ds(CAP * d, CAP)]
        return remote(part, part, dpr.at[0], dp=z_peer(i))

    def ycopy(i):
        part = dsl.at[pl.ds(CAP * nz * y, CAP * nz)]
        return remote(part, part, dpr.at[1], dp=y_peer(i))

    z_order = sorted(range(nz), key=lambda o: -min(o, nz - o))
    part_slots = CAP * nz // 2

    def gycopy(i, part):
        some = pl.ds(part * part_slots, part_slots)
        return remote(gsl.at[i, some], gy.at[i - 1, some], dpr.at[2 + part], dp=y_peer(i))

    def gzcopy(p):
        return remote(gys.at[pl.ds(CAP * p, CAP)], gz.at[p], dpr.at[4], dp=z_peer(z_order[p]))

    def rs_sib(j):
        return remote(sibs.at[j], sibr.at[j], rsr.at[0], tensor=t_sib)

    def rs_one(j):
        return (
            remote(s1s.at[j, 0], s1r.at[j, 0], rsr.at[1 + lax.div(j, 4)], tensor=t_right),
            remote(s1s.at[j, 1], s1r.at[j, 1], rsr.at[1 + lax.div(j, 4)], tensor=t_left),
        )

    def rs_two(j):
        return (
            remote(s2s.at[j, 0], s2r.at[j, 0], rsr.at[3], tensor=t_right),
            remote(s2s.at[j, 1], s2r.at[j, 1], rsr.at[3], tensor=t_left),
        )

    tell()
    for q in range(6):
        ag_own(q)

    own_delta.wait()
    entries = dlv[...].astype(F32)
    for s in range(CAP):
        rows = [entries[s : s + 1, i * HD : (i + 1) * HD] for i in range(ROWS)]
        dsl[CAP * d + s] = jnp.concatenate(rows, axis=0).astype(BF16)
    gc[NB] = jnp.zeros((ROWS, HD), F32)

    own_og.wait()
    order = [at(dx, core) for core in (c, 1 - c) for dx in (0, 1, 3, 2)]
    for i, k in enumerate(order):
        ogp[pl.ds(i * ROWS, ROWS), :] = ogf[t, pl.ds(pl.multiple_of(k * ROWS, ROWS), ROWS), :]
    pl.semaphore_wait(known, len(along))
    for i in sorted(range(1, nz), key=lambda o: -min(o, nz - o)):
        zcopy(i).start()

    def backward(i, _):
        rows = pl.ds(pl.multiple_of(i * CW, CW), CW)
        part = lax.dot_general(
            ogp[...], wv[rows, :], (((1,), (1,)), ((), ())), preferred_element_type=F32
        )
        sibs[i] = part[4 * ROWS :].astype(BF16)
        pown[i] = part[: 4 * ROWS]
        rs_sib(i).start()
        return 0

    for j in range(4):
        w_copies[j].wait()
        lax.fori_loop(2 * j, 2 * j + 2, backward, 0)
        ag_pass(j)
        if j == 2:
            wait_kb(dpr.at[0], (nz - 1) * KB)
            for i in sorted(range(1, ny), key=lambda o: -min(o, ny - o)):
                ycopy(i).start()

    own_owner.wait()
    owners = [owner[b] for b in range(NB)]
    lane = lax.broadcasted_iota(jnp.int32, (1, HD), 1)
    holds = jnp.full((1, HD), NB, jnp.int32)
    for b in range(NB):
        place = CAP * owners[b]
        for before in range(b):
            place = place + (owners[before] == owners[b]).astype(jnp.int32)
        slot[b] = place
        holds = jnp.where(lane == place, b, holds)
    blkv[...] = holds
    to_smem = pltpu.make_async_copy(blkv, blk, lsem.at[3])
    to_smem.start()

    def pair_sum(j, _):
        total = pown[j] + sibr[j].astype(F32)
        qs[j] = total[:ROWS]
        qr[j] = total[ROWS : 2 * ROWS]
        ql[j] = total[2 * ROWS : 3 * ROWS]
        far = total[3 * ROWS :].astype(BF16)
        s1s[j, 0] = far[:, :HALF]
        s1s[j, 1] = far[:, HALF:]
        return 0

    ag_pass(4)
    ag_pass(5)
    wait_kb(rsr.at[0], CHUNKS * 128)
    lax.fori_loop(0, CHUNKS, pair_sum, 0)

    def send_one(j, _):
        for copy in rs_one(j):
            copy.start()
        return 0

    lax.fori_loop(0, CHUNKS, send_one, 0)
    wait_kb(dpr.at[1], (ny - 1) * nz * KB)
    for b in range(NB):
        dcp[b, pl.ds(t * ROWS, ROWS), :] = dsl[slot[b]]
    ag_own(6)
    ag_own(7)
    own_tok.wait()
    own_index.wait()

    pick_row = lax.broadcasted_iota(jnp.int32, (ROWS, HD), 0) + t * ROWS
    pick = (pick_row == lax.broadcasted_iota(jnp.int32, (ROWS, HD), 1)).astype(BF16)

    def arrange(q):
        wait_kb(sbr.at[q], 4 * 64)
        if q < 2:
            for h in range(NT * HEADS_DEV):
                col = h % HEADS_DEV * HD
                some = slice(64 * q, 64 * q + 64)
                og3[h, some, :] = ogf[h // HEADS_DEV, some, col : col + HD]
                if q == 1:
                    og16[h] = og3[h, pl.ds(pl.multiple_of(t * ROWS, ROWS), ROWS), :]
        else:
            for r in range(16 * (q - 2), 16 * (q - 1)):
                slab = tokf[:, r * HD : (r + 1) * HD]
                tok3[r] = slab
                tokt[r] = lax.dot_general(
                    pick, slab, (((1,), (1,)), ((), ())), preferred_element_type=F32
                ).astype(BF16)

    ag_last(0)
    ag_last(1)
    ag_last(2)
    ag_last(3)
    arrange(0)
    arrange(1)
    ag_last(4)
    ag_last(5)
    for q in range(2, 6):
        arrange(q)

    for b in range(NB):
        gc[b] = jnp.dot(tokt[index[0, b]], og3[index[1, b]], preferred_element_type=F32) * grad_scale
    to_smem.wait()
    for i in range(ny):
        for p, o in enumerate(z_order):
            for s in range(CAP):
                place = CAP * (y_peer(i) - z + lax.rem(z + o, nz)) + s
                gsl[i, CAP * p + s] = gc[blk[0, place]].astype(BF16)
    for part in range(2):
        for i in sorted(range(1, ny), key=lambda o: -min(o, ny - o)):
            gycopy(i, part).start()

    def send_two(j, _):
        s2s[j, 0, :, :HALF] = (qr[j, :, :HALF] + s1r[j, 0].astype(F32)).astype(BF16)
        s2s[j, 0, :, HALF:] = qr[j, :, HALF:].astype(BF16)
        s2s[j, 1, :, :HALF] = ql[j, :, :HALF].astype(BF16)
        s2s[j, 1, :, HALF:] = (ql[j, :, HALF:] + s1r[j, 1].astype(F32)).astype(BF16)
        for copy in rs_two(j):
            copy.start()
        return 0

    for b in range(NB):
        lhs[:, b * HD : (b + 1) * HD] = tok3[index[0, b]]
    ag_pass(6)
    ag_pass(7)
    for half in range(2):
        wait_kb(rsr.at[1 + half], 128)
        lax.fori_loop(4 * half, 4 * half + 4, send_two, 0)

    proj[...] = jnp.zeros_like(proj)

    def forward(i, _):
        rows = pl.ds(pl.multiple_of(i * CW, CW), CW)
        proj[...] += jnp.dot(tokf[:, rows], wv[rows, :], preferred_element_type=F32)
        return 0

    lax.fori_loop(0, CHUNKS, forward, 0)

    def delta_terms(g, _):
        for i in range(0, 8, 2):
            ends, parts = [], []
            for k in (i, i + 1):
                b = g * 8 + k
                head = index[1, b]
                block = dcp[b]
                for h in range(HEADS_DEV):
                    keep = jnp.where(head == t * HEADS_DEV + h, 1.0, 0.0)
                    keep = jnp.full((1, HD), keep, F32).astype(BF16)
                    rhs[k * HD : (k + 1) * HD, h * HD : (h + 1) * HD] = block * keep
                ends.append(og16[head])
                parts.append(block)
            both = lax.dot_general(
                jnp.concatenate(ends, axis=0), jnp.concatenate(parts, axis=0),
                (((1,), (1,)), ((), ())), preferred_element_type=F32,
            )
            udel[g * 8 + i] = both[:ROWS, :HD]
            udel[g * 8 + i + 1] = both[ROWS:, HD:]
        some = pl.ds(pl.multiple_of(g * 8 * HD, HD), 8 * HD)
        proj[...] += jnp.dot(lhs[:, some], rhs[...], preferred_element_type=F32)
        return 0

    ag_last(6)
    ag_last(7)
    for part in range(2):
        wait_kb(dpr.at[2 + part], (ny - 1) * nz * KB // 2)
        for p in range(part * nz // 2, (part + 1) * nz // 2):
            for s in range(CAP * p, CAP * (p + 1)):
                total = gsl[0, s].astype(F32)
                for i in range(ny - 1):
                    total = total + gy[i, s].astype(F32)
                gys[s] = total.astype(BF16)
        for p in range(part * nz // 2, (part + 1) * nz // 2):
            if p < nz - 1:
                gzcopy(p).start()

    wait_kb(sbr.at[6], 4 * 64)
    lax.fori_loop(0, 2, delta_terms, 0)
    wait_kb(sbr.at[7], 4 * 64)
    lax.fori_loop(2, 4, delta_terms, 0)

    def last_sum(j, _):
        out = qs[j] + s2r[j, 0].astype(F32) + s2r[j, 1].astype(F32)
        igb[:, pl.ds(pl.multiple_of(j * CW, CW), CW)] = out
        return 0

    wait_kb(rsr.at[3], CHUNKS * 64)
    lax.fori_loop(0, CHUNKS, last_sum, 0)

    wait_kb(dpr.at[4], (nz - 1) * KB)
    for s in range(CAP):
        total = gys[CAP * (nz - 1) + s].astype(F32)
        for i in range(nz - 1):
            total = total + gz[i, s].astype(F32)
        grad_out[s : s + 1, :] = jnp.concatenate([total[i : i + 1] for i in range(ROWS)], axis=1)

    sent = (8 * 7 * 64) + CHUNKS * (128 + 32 + 64) + 2 * (nz - 1) * KB + 2 * (ny - 1) * nz * KB
    part = wv.at[pl.ds(0, sent)]
    remote(part, part, rsr.at[0], tensor=t_sib).wait_send()


def last_kernel(index, igb, udel, proj, grad, dl, m1, m2, proj_out, ig_out, nd, nm1, nm2, total):
    total[...] = igb[...]
    for b in range(NB):
        here = pl.ds(pl.multiple_of(index[0, b] * HD, HD), HD)
        total[:, here] += udel[b]
    ig_out[...] = total[...].astype(BF16)
    proj_out[...] = proj[...].astype(BF16)
    g = grad[...]
    first = 0.9 * m1[...] + 0.1 * g
    second = 0.999 * m2[...] + 0.001 * g * g
    step = 0.02 * (first / CORRECT_ONE) / (jnp.sqrt(second / CORRECT_TWO) + 1e-08)
    nm1[...] = first
    nm2[...] = second
    nd[...] = (dl[...].astype(F32) - step).astype(BF16)


def on_device(ny, nz, tokens, base_weight, out_grad, block_index, block_owner, delta, moment1, moment2):
    slots = CAP * ny * nz
    smem = pl.BlockSpec(memory_space=pltpu.SMEM)
    vmem = pl.BlockSpec(memory_space=pltpu.VMEM)
    hbm = pl.BlockSpec(memory_space=pltpu.HBM)
    index = block_index.T
    dma = pltpu.SemaphoreType.DMA
    grad_scale = 1.0 / math.sqrt(TOK * ny * nz)
    shape = jax.ShapeDtypeStruct

    igb, udel, proj, grad = pl.pallas_call(
        lambda *refs: step_kernel(ny, nz, grad_scale, *refs),
        out_shape=(
            shape((ROWS, D), F32),
            shape((NB, ROWS, HD), F32),
            shape((TOK, WIDTH), F32),
            shape(delta.shape, F32),
        ),
        in_specs=[hbm] * 6,
        out_specs=(vmem,) * 4,
        scratch_shapes=[
            pltpu.VMEM((D, WIDTH), BF16),
            pltpu.VMEM((TOK, D), BF16),
            pltpu.VMEM((D // HD, TOK, HD), BF16),
            pltpu.VMEM((D // HD, ROWS, HD), BF16),
            pltpu.VMEM((NT, TOK, WIDTH), BF16),
            pltpu.VMEM((NT * HEADS_DEV, TOK, HD), BF16),
            pltpu.VMEM((NT * HEADS_DEV, ROWS, HD), BF16),
            pltpu.VMEM((TOK, WIDTH), BF16),
            pltpu.VMEM(delta.shape, BF16),
            pltpu.VMEM((slots, ROWS, HD), BF16),
            pltpu.VMEM((NB, HD, HD), BF16),
            pltpu.VMEM((NB + 1, ROWS, HD), F32),
            pltpu.VMEM((ny, CAP * nz, ROWS, HD), BF16),
            pltpu.VMEM((ny - 1, CAP * nz, ROWS, HD), BF16),
            pltpu.VMEM((CAP * nz, ROWS, HD), BF16),
            pltpu.VMEM((nz - 1, CAP, ROWS, HD), BF16),
            pltpu.VMEM((CHUNKS, 4 * ROWS, CW), F32),
            pltpu.VMEM((CHUNKS, 4 * ROWS, CW), BF16),
            pltpu.VMEM((CHUNKS, 4 * ROWS, CW), BF16),
            pltpu.VMEM((CHUNKS, 2, ROWS, HALF), BF16),
            pltpu.VMEM((CHUNKS, 2, ROWS, HALF), BF16),
            pltpu.VMEM((CHUNKS, 2, ROWS, CW), BF16),
            pltpu.VMEM((CHUNKS, 2, ROWS, CW), BF16),
            pltpu.VMEM((CHUNKS, ROWS, CW), F32),
            pltpu.VMEM((CHUNKS, ROWS, CW), F32),
            pltpu.VMEM((CHUNKS, ROWS, CW), F32),
            pltpu.VMEM((TOK, NB * HD), BF16),
            pltpu.VMEM((8 * HD, WIDTH), BF16),
            pltpu.VMEM((1, HD), jnp.int32),
            pltpu.SMEM((1, HD), jnp.int32),
            pltpu.SMEM((NB,), jnp.int32),
            pltpu.SMEM((2, NB), jnp.int32),
            pltpu.SMEM((NB,), jnp.int32),
            dma((4,)),
            dma((6,)),
            dma,
            dma((8, 3)),
            dma((8,)),
            dma((5,)),
            dma((4,)),
            pltpu.SemaphoreType.REGULAR,
        ],
        compiler_params=pltpu.CompilerParams(
            collective_id=0, has_side_effects=True, vmem_limit_bytes=50 * 1024 * 1024
        ),
        name="step",
    )(*(pltpu.with_memory_space_constraint(a, pltpu.HBM) for a in (index, block_owner, tokens, base_weight, out_grad, delta)))

    return pl.pallas_call(
        last_kernel,
        out_shape=(
            shape((TOK, WIDTH), BF16),
            shape((ROWS, D), BF16),
            shape(delta.shape, BF16),
            shape(delta.shape, F32),
            shape(delta.shape, F32),
        ),
        in_specs=[smem] + [vmem] * 7,
        out_specs=(vmem,) * 5,
        scratch_shapes=[pltpu.VMEM((ROWS, D), F32)],
        compiler_params=pltpu.CompilerParams(vmem_limit_bytes=8 * 1024 * 1024),
        name="last",
    )(index, igb, udel, proj, grad, delta, moment1, moment2)


def solution(mesh):
    dp = mesh.shape["dp"]
    nz = 8
    ny = dp // nz

    def per_device(*args):
        return on_device(ny, nz, *args)

    both = P("dp", "tensor")
    rows = P(("dp", "tensor"), None)
    return jax.shard_map(
        per_device,
        mesh=mesh,
        in_specs=(rows, P(None, "tensor"), both, P(), P(), both, both, both),
        out_specs=(both, rows, both, both, both),
        check_vma=False,
    )
```

```python
import math

import jax
import jax.numpy as jnp
from jax import lax
from jax.experimental import pallas as pl
from jax.experimental.pallas import tpu as pltpu
from jax.sharding import PartitionSpec as P

D = 8192
HD = 128
NB = 32
CAP = 2
NX = 4
NT = 8
ROWS = 16
TOK = 128
WIDTH = 512
HEADS_DEV = 4
CHUNKS = 8
CW = D // CHUNKS
HALF = CW // 2
KB = 8

CORRECT_ONE = 1.0 - 0.9**10
CORRECT_TWO = 1.0 - 0.999**10

F32 = jnp.float32
BF16 = jnp.bfloat16
MESH = pl.DeviceIdType.MESH


def step_kernel(
    ny, nz, grad_scale,
    index_in, owner_in, tok, wt, og, dl,
    igb, udel, proj, grad_out,
    wv, tokf, tok3, tokt, ogf, og3, og16, ogp, dlv, dsl, dcp, gc, gsl, gy, gys, gz,
    pown, sibs, sibr, s1s, s1r, s2s, s2r, qs, qr, ql, lhs, rhs, blkv, blk, slot, index, owner,
    wsem, lsem, snd, agr, sbr, dpr, rsr, known,
):
    d = lax.axis_index("dp")
    t = lax.axis_index("tensor")
    y, z = lax.div(d, nz), lax.rem(d, nz)
    x, c = lax.div(t, 2), lax.rem(t, 2)

    def at(dx, core):
        return lax.rem(x + dx, NX) * 2 + core

    t_right, t_left, t_opp, t_sib = at(1, c), at(3, c), at(2, c), at(0, 1 - c)

    def z_peer(i):
        return y * nz + lax.rem(z + i, nz)

    def y_peer(i):
        return lax.rem(y + i, ny) * nz + z

    def remote(src, dst, recv, **where):
        return pltpu.make_async_remote_copy(
            src_ref=src, dst_ref=dst, send_sem=snd, recv_sem=recv,
            device_id=where, device_id_type=MESH,
        )

    def wait_kb(sem, kb):
        part = wv.at[pl.ds(0, kb)]
        remote(part, part, sem, tensor=t_sib).wait_recv()

    own_delta = pltpu.make_async_copy(dl, dlv, lsem.at[0])
    own_og = pltpu.make_async_copy(og, ogf.at[t], lsem.at[1])
    own_tok = pltpu.make_async_copy(tok, tokf.at[pl.ds(t * ROWS, ROWS), :], lsem.at[2])
    own_index = pltpu.make_async_copy(index_in, index, lsem.at[4])
    own_owner = pltpu.make_async_copy(owner_in, owner, lsem.at[5])
    own_owner.start()
    own_index.start()
    own_delta.start()
    own_og.start()
    w_copies = []
    for j in range(4):
        part = pl.ds(j * (D // 4), D // 4)
        w_copies.append(pltpu.make_async_copy(wt.at[part, :], wv.at[part, :], wsem.at[j]))
        w_copies[j].start()
    own_tok.start()

    barrier = pltpu.get_barrier_semaphore()
    along = [{"dp": z_peer(2)}, {"dp": z_peer(nz - 2)}, {"dp": y_peer(1)}, {"dp": y_peer(ny - 1)}]
    near = [{"tensor": t_right}, {"tensor": t_left}, {"tensor": t_sib}] + along
    near += [{"dp": z_peer(1)}, {"dp": z_peer(nz - 1)}]
    for where in near:
        pl.semaphore_signal(barrier, inc=1, device_id=where, device_id_type=MESH)

    pl.semaphore_wait(barrier, len(near))

    def tell():
        for where in along:
            pl.semaphore_signal(known, inc=1, device_id=where, device_id_type=MESH)

    def shard(q, k):
        if q < 2:
            return ogf.at[k, pl.ds(64 * q, 64), :]
        if q < 6:
            return tokf.at[pl.ds(k * ROWS, ROWS), pl.ds(2048 * (q - 2), 2048)]
        return dcp.at[pl.ds(16 * (q - 6), 16), pl.ds(k * ROWS, ROWS), :]

    def mine(q):
        if q < 2:
            return og.at[pl.ds(64 * q, 64), :]
        if q < 6:
            return tok.at[:, pl.ds(2048 * (q - 2), 2048)]
        return shard(q, t)

    def ag(q, kind):
        sib = sbr.at[q]
        if kind == 0:
            return remote(mine(q), shard(q, t), agr.at[q, 0], tensor=t_right)
        if kind == 1:
            return remote(mine(q), shard(q, t), agr.at[q, 1], tensor=t_left)
        if kind == 2:
            return remote(mine(q), shard(q, t), sib, tensor=t_sib)
        if kind == 3:
            return remote(shard(q, t_left), shard(q, t_left), sib, tensor=t_sib)
        if kind == 4:
            return remote(shard(q, t_right), shard(q, t_right), sib, tensor=t_sib)
        if kind == 5 and q % 2 == 0:
            return remote(shard(q, t_left), shard(q, t_left), agr.at[q, 2], tensor=t_right)
        if kind == 5:
            return remote(shard(q, t_right), shard(q, t_right), agr.at[q, 2], tensor=t_left)
        return remote(shard(q, t_opp), shard(q, t_opp), sib, tensor=t_sib)

    def ag_own(q):
        for kind in range(3):
            ag(q, kind).start()

    def ag_pass(q):
        far = q % 2
        ag(q, far).wait_recv()
        ag(q, 5).start()
        ag(q, 3 + far).start()
        ag(q, 1 - far).wait_recv()
        ag(q, 4 - far).start()

    def ag_last(q):
        ag(q, 5).wait_recv()
        ag(q, 6).start()

    def zcopy(i):
        part = dsl.at[pl.ds(CAP * d, CAP)]
        return remote(part, part, dpr.at[0], dp=z_peer(i))

    def ycopy(i):
        part = dsl.at[pl.ds(CAP * nz * y, CAP * nz)]
        return remote(part, part, dpr.at[1], dp=y_peer(i))

    z_order = sorted(range(nz), key=lambda o: -min(o, nz - o))
    part_slots = CAP * nz // 2

    def gycopy(i, part):
        some = pl.ds(part * part_slots, part_slots)
        return remote(gsl.at[i, some], gy.at[i - 1, some], dpr.at[2 + part], dp=y_peer(i))

    def gzcopy(p):
        return remote(gys.at[pl.ds(CAP * p, CAP)], gz.at[p], dpr.at[4], dp=z_peer(z_order[p]))

    def rs_sib(j):
        return remote(sibs.at[j], sibr.at[j], rsr.at[0], tensor=t_sib)

    def rs_one(j):
        return (
            remote(s1s.at[j, 0], s1r.at[j, 0], rsr.at[1 + lax.div(j, 4)], tensor=t_right),
            remote(s1s.at[j, 1], s1r.at[j, 1], rsr.at[1 + lax.div(j, 4)], tensor=t_left),
        )

    def rs_two(j):
        return (
            remote(s2s.at[j, 0], s2r.at[j, 0], rsr.at[3], tensor=t_right),
            remote(s2s.at[j, 1], s2r.at[j, 1], rsr.at[3], tensor=t_left),
        )

    tell()
    for q in range(6):
        ag_own(q)

    own_delta.wait()
    entries = dlv[...].astype(F32)
    for s in range(CAP):
        rows = [entries[s : s + 1, i * HD : (i + 1) * HD] for i in range(ROWS)]
        dsl[CAP * d + s] = jnp.concatenate(rows, axis=0).astype(BF16)
    gc[NB] = jnp.zeros((ROWS, HD), F32)

    own_og.wait()
    order = [at(dx, core) for core in (c, 1 - c) for dx in (0, 1, 3, 2)]
    for i, k in enumerate(order):
        ogp[pl.ds(i * ROWS, ROWS), :] = ogf[t, pl.ds(pl.multiple_of(k * ROWS, ROWS), ROWS), :]
    pl.semaphore_wait(known, len(along))
    for i in sorted(range(1, nz), key=lambda o: -min(o, nz - o)):
        zcopy(i).start()

    def backward(i, _):
        rows = pl.ds(pl.multiple_of(i * CW, CW), CW)
        part = lax.dot_general(
            ogp[...], wv[rows, :], (((1,), (1,)), ((), ())), preferred_element_type=F32
        )
        sibs[i] = part[4 * ROWS :].astype(BF16)
        pown[i] = part[: 4 * ROWS]
        rs_sib(i).start()
        return 0

    for j in range(4):
        w_copies[j].wait()
        lax.fori_loop(2 * j, 2 * j + 2, backward, 0)
        ag_pass(j)
        if j == 2:
            wait_kb(dpr.at[0], (nz - 1) * KB)
            for i in sorted(range(1, ny), key=lambda o: -min(o, ny - o)):
                ycopy(i).start()

    own_owner.wait()
    owners = [owner[b] for b in range(NB)]
    lane = lax.broadcasted_iota(jnp.int32, (1, HD), 1)
    holds = jnp.full((1, HD), NB, jnp.int32)
    for b in range(NB):
        place = CAP * owners[b]
        for before in range(b):
            place = place + (owners[before] == owners[b]).astype(jnp.int32)
        slot[b] = place
        holds = jnp.where(lane == place, b, holds)
    blkv[...] = holds
    to_smem = pltpu.make_async_copy(blkv, blk, lsem.at[3])
    to_smem.start()

    def pair_sum(j, _):
        total = pown[j] + sibr[j].astype(F32)
        qs[j] = total[:ROWS]
        qr[j] = total[ROWS : 2 * ROWS]
        ql[j] = total[2 * ROWS : 3 * ROWS]
        far = total[3 * ROWS :].astype(BF16)
        s1s[j, 0] = far[:, :HALF]
        s1s[j, 1] = far[:, HALF:]
        return 0

    ag_pass(4)
    ag_pass(5)
    wait_kb(rsr.at[0], CHUNKS * 128)
    lax.fori_loop(0, CHUNKS, pair_sum, 0)

    def send_one(j, _):
        for copy in rs_one(j):
            copy.start()
        return 0

    lax.fori_loop(0, CHUNKS, send_one, 0)
    own_tok.wait()
    own_index.wait()

    pick_row = lax.broadcasted_iota(jnp.int32, (ROWS, HD), 0) + t * ROWS
    pick = (pick_row == lax.broadcasted_iota(jnp.int32, (ROWS, HD), 1)).astype(BF16)

    def arrange(q):
        wait_kb(sbr.at[q], 4 * 64)
        if q < 2:
            for h in range(NT * HEADS_DEV):
                col = h % HEADS_DEV * HD
                some = slice(64 * q, 64 * q + 64)
                og3[h, some, :] = ogf[h // HEADS_DEV, some, col : col + HD]
                if q == 1:
                    og16[h] = og3[h, pl.ds(pl.multiple_of(t * ROWS, ROWS), ROWS), :]
        else:
            for r in range(16 * (q - 2), 16 * (q - 1)):
                slab = tokf[:, r * HD : (r + 1) * HD]
                tok3[r] = slab
                tokt[r] = lax.dot_general(
                    pick, slab, (((1,), (1,)), ((), ())), preferred_element_type=F32
                ).astype(BF16)

    ag_last(0)
    ag_last(1)
    wait_kb(dpr.at[1], (ny - 1) * nz * KB)
    for b in range(NB):
        dcp[b, pl.ds(t * ROWS, ROWS), :] = dsl[slot[b]]
    ag_own(6)
    ag_own(7)
    ag_last(2)
    ag_last(3)
    arrange(0)
    arrange(1)
    ag_last(4)
    ag_last(5)
    for q in range(2, 6):
        arrange(q)

    for b in range(NB):
        gc[b] = jnp.dot(tokt[index[0, b]], og3[index[1, b]], preferred_element_type=F32) * grad_scale
    to_smem.wait()
    for i in range(ny):
        for p, o in enumerate(z_order):
            for s in range(CAP):
                place = CAP * (y_peer(i) - z + lax.rem(z + o, nz)) + s
                gsl[i, CAP * p + s] = gc[blk[0, place]].astype(BF16)
    for part in range(2):
        for i in sorted(range(1, ny), key=lambda o: -min(o, ny - o)):
            gycopy(i, part).start()

    def send_two(j, _):
        s2s[j, 0, :, :HALF] = (qr[j, :, :HALF] + s1r[j, 0].astype(F32)).astype(BF16)
        s2s[j, 0, :, HALF:] = qr[j, :, HALF:].astype(BF16)
        s2s[j, 1, :, :HALF] = ql[j, :, :HALF].astype(BF16)
        s2s[j, 1, :, HALF:] = (ql[j, :, HALF:] + s1r[j, 1].astype(F32)).astype(BF16)
        for copy in rs_two(j):
            copy.start()
        return 0

    for b in range(NB):
        lhs[:, b * HD : (b + 1) * HD] = tok3[index[0, b]]
    ag_pass(6)
    ag_pass(7)
    for half in range(2):
        wait_kb(rsr.at[1 + half], 128)
        lax.fori_loop(4 * half, 4 * half + 4, send_two, 0)

    proj[...] = jnp.zeros_like(proj)

    def forward(i, _):
        rows = pl.ds(pl.multiple_of(i * CW, CW), CW)
        proj[...] += jnp.dot(tokf[:, rows], wv[rows, :], preferred_element_type=F32)
        return 0

    lax.fori_loop(0, CHUNKS, forward, 0)

    def delta_terms(g, _):
        for i in range(0, 8, 2):
            ends, parts = [], []
            for k in (i, i + 1):
                b = g * 8 + k
                head = index[1, b]
                block = dcp[b]
                for h in range(HEADS_DEV):
                    keep = jnp.where(head == t * HEADS_DEV + h, 1.0, 0.0)
                    keep = jnp.full((1, HD), keep, F32).astype(BF16)
                    rhs[k * HD : (k + 1) * HD, h * HD : (h + 1) * HD] = block * keep
                ends.append(og16[head])
                parts.append(block)
            both = lax.dot_general(
                jnp.concatenate(ends, axis=0), jnp.concatenate(parts, axis=0),
                (((1,), (1,)), ((), ())), preferred_element_type=F32,
            )
            udel[g * 8 + i] = both[:ROWS, :HD]
            udel[g * 8 + i + 1] = both[ROWS:, HD:]
        some = pl.ds(pl.multiple_of(g * 8 * HD, HD), 8 * HD)
        proj[...] += jnp.dot(lhs[:, some], rhs[...], preferred_element_type=F32)
        return 0

    ag_last(6)
    ag_last(7)
    for part in range(2):
        wait_kb(dpr.at[2 + part], (ny - 1) * nz * KB // 2)
        for p in range(part * nz // 2, (part + 1) * nz // 2):
            for s in range(CAP * p, CAP * (p + 1)):
                total = gsl[0, s].astype(F32)
                for i in range(ny - 1):
                    total = total + gy[i, s].astype(F32)
                gys[s] = total.astype(BF16)
        for p in range(part * nz // 2, (part + 1) * nz // 2):
            if p < nz - 1:
                gzcopy(p).start()

    wait_kb(sbr.at[6], 4 * 64)
    lax.fori_loop(0, 2, delta_terms, 0)
    wait_kb(sbr.at[7], 4 * 64)
    lax.fori_loop(2, 4, delta_terms, 0)

    def last_sum(j, _):
        out = qs[j] + s2r[j, 0].astype(F32) + s2r[j, 1].astype(F32)
        igb[:, pl.ds(pl.multiple_of(j * CW, CW), CW)] = out
        return 0

    wait_kb(rsr.at[3], CHUNKS * 64)
    lax.fori_loop(0, CHUNKS, last_sum, 0)

    wait_kb(dpr.at[4], (nz - 1) * KB)
    for s in range(CAP):
        total = gys[CAP * (nz - 1) + s].astype(F32)
        for i in range(nz - 1):
            total = total + gz[i, s].astype(F32)
        grad_out[s : s + 1, :] = jnp.concatenate([total[i : i + 1] for i in range(ROWS)], axis=1)

    sent = (8 * 7 * 64) + CHUNKS * (128 + 32 + 64) + 2 * (nz - 1) * KB + 2 * (ny - 1) * nz * KB
    part = wv.at[pl.ds(0, sent)]
    remote(part, part, rsr.at[0], tensor=t_sib).wait_send()


def last_kernel(index, igb, udel, proj, grad, dl, m1, m2, proj_out, ig_out, nd, nm1, nm2, total):
    total[...] = igb[...]
    for b in range(NB):
        here = pl.ds(pl.multiple_of(index[0, b] * HD, HD), HD)
        total[:, here] += udel[b]
    ig_out[...] = total[...].astype(BF16)
    proj_out[...] = proj[...].astype(BF16)
    g = grad[...]
    first = 0.9 * m1[...] + 0.1 * g
    second = 0.999 * m2[...] + 0.001 * g * g
    step = 0.02 * (first / CORRECT_ONE) / (jnp.sqrt(second / CORRECT_TWO) + 1e-08)
    nm1[...] = first
    nm2[...] = second
    nd[...] = (dl[...].astype(F32) - step).astype(BF16)


def on_device(ny, nz, tokens, base_weight, out_grad, block_index, block_owner, delta, moment1, moment2):
    slots = CAP * ny * nz
    smem = pl.BlockSpec(memory_space=pltpu.SMEM)
    vmem = pl.BlockSpec(memory_space=pltpu.VMEM)
    hbm = pl.BlockSpec(memory_space=pltpu.HBM)
    index = block_index.T
    dma = pltpu.SemaphoreType.DMA
    grad_scale = 1.0 / math.sqrt(TOK * ny * nz)
    shape = jax.ShapeDtypeStruct

    igb, udel, proj, grad = pl.pallas_call(
        lambda *refs: step_kernel(ny, nz, grad_scale, *refs),
        out_shape=(
            shape((ROWS, D), F32),
            shape((NB, ROWS, HD), F32),
            shape((TOK, WIDTH), F32),
            shape(delta.shape, F32),
        ),
        in_specs=[hbm] * 6,
        out_specs=(vmem,) * 4,
        scratch_shapes=[
            pltpu.VMEM((D, WIDTH), BF16),
            pltpu.VMEM((TOK, D), BF16),
            pltpu.VMEM((D // HD, TOK, HD), BF16),
            pltpu.VMEM((D // HD, ROWS, HD), BF16),
            pltpu.VMEM((NT, TOK, WIDTH), BF16),
            pltpu.VMEM((NT * HEADS_DEV, TOK, HD), BF16),
            pltpu.VMEM((NT * HEADS_DEV, ROWS, HD), BF16),
            pltpu.VMEM((TOK, WIDTH), BF16),
            pltpu.VMEM(delta.shape, BF16),
            pltpu.VMEM((slots, ROWS, HD), BF16),
            pltpu.VMEM((NB, HD, HD), BF16),
            pltpu.VMEM((NB + 1, ROWS, HD), F32),
            pltpu.VMEM((ny, CAP * nz, ROWS, HD), BF16),
            pltpu.VMEM((ny - 1, CAP * nz, ROWS, HD), BF16),
            pltpu.VMEM((CAP * nz, ROWS, HD), BF16),
            pltpu.VMEM((nz - 1, CAP, ROWS, HD), BF16),
            pltpu.VMEM((CHUNKS, 4 * ROWS, CW), F32),
            pltpu.VMEM((CHUNKS, 4 * ROWS, CW), BF16),
            pltpu.VMEM((CHUNKS, 4 * ROWS, CW), BF16),
            pltpu.VMEM((CHUNKS, 2, ROWS, HALF), BF16),
            pltpu.VMEM((CHUNKS, 2, ROWS, HALF), BF16),
            pltpu.VMEM((CHUNKS, 2, ROWS, CW), BF16),
            pltpu.VMEM((CHUNKS, 2, ROWS, CW), BF16),
            pltpu.VMEM((CHUNKS, ROWS, CW), F32),
            pltpu.VMEM((CHUNKS, ROWS, CW), F32),
            pltpu.VMEM((CHUNKS, ROWS, CW), F32),
            pltpu.VMEM((TOK, NB * HD), BF16),
            pltpu.VMEM((8 * HD, WIDTH), BF16),
            pltpu.VMEM((1, HD), jnp.int32),
            pltpu.SMEM((1, HD), jnp.int32),
            pltpu.SMEM((NB,), jnp.int32),
            pltpu.SMEM((2, NB), jnp.int32),
            pltpu.SMEM((NB,), jnp.int32),
            dma((4,)),
            dma((6,)),
            dma,
            dma((8, 3)),
            dma((8,)),
            dma((5,)),
            dma((4,)),
            pltpu.SemaphoreType.REGULAR,
        ],
        compiler_params=pltpu.CompilerParams(
            collective_id=0, has_side_effects=True, vmem_limit_bytes=50 * 1024 * 1024
        ),
        name="step",
    )(*(pltpu.with_memory_space_constraint(a, pltpu.HBM) for a in (index, block_owner, tokens, base_weight, out_grad, delta)))

    return pl.pallas_call(
        last_kernel,
        out_shape=(
            shape((TOK, WIDTH), BF16),
            shape((ROWS, D), BF16),
            shape(delta.shape, BF16),
            shape(delta.shape, F32),
            shape(delta.shape, F32),
        ),
        in_specs=[smem] + [vmem] * 7,
        out_specs=(vmem,) * 5,
        scratch_shapes=[pltpu.VMEM((ROWS, D), F32)],
        compiler_params=pltpu.CompilerParams(vmem_limit_bytes=8 * 1024 * 1024),
        name="last",
    )(index, igb, udel, proj, grad, delta, moment1, moment2)


def solution(mesh):
    dp = mesh.shape["dp"]
    nz = 8
    ny = dp // nz

    def per_device(*args):
        return on_device(ny, nz, *args)

    both = P("dp", "tensor")
    rows = P(("dp", "tensor"), None)
    return jax.shard_map(
        per_device,
        mesh=mesh,
        in_specs=(rows, P(None, "tensor"), both, P(), P(), both, both, both),
        out_specs=(both, rows, both, both, both),
        check_vma=False,
    )
```
